32 devices in a mesh: grp: 2 (over x), chan: 16 (over z, y, core).
Axes of the slice: x: 2, y: 2, z: 4, core: 2. Of those that a mesh axis runs over, the one named last changes fastest.
Arguments:
- voltages: bfloat16 [2, 1024, 2, 32, 512], P(None, 'chan', None, None, 'grp'), parts along dimension 4, may hold values from -80 to 80
- gains: float32 [2, 2, 1024], P(None, None, 'chan'), may hold values from -1 to 1
- feed_cyl: int32 [1024], replicated, may hold values from 0 to 3, as said below
- feed_ns: int32 [1024], replicated, may hold values from 0 to 255
- ew_index: int32 [4, 4], replicated, may hold values from 0 to 63
- ns_beam: int32 [256], replicated, may hold values from 0 to 511
Outputs:
- intensity: float32 [1024, 8, 512], P('chan', 'grp'), parts along dimension 1
The draws below stay inside these ranges and needn't reach their ends.
There are 2 independent parts, one for each index of `grp`. The reference program is written for one: setup_inputs(seed, part) draws one part's arguments, and reference() takes and returns one part's arrays. A program takes and returns all parts, laid end to end along the dimension named above; an argument that names none is the same for every part. Nothing has to cross between parts.
Inputs may be any that keep to these rules, and one draw needn't show every extreme that they name: Together, feed_cyl and feed_ns name every pair of a cylinder and a north-south position exactly once.
All inputs are finite; a program needn't handle non-finite values.
Results may differ from the reference program's by a relative error of at most 0.0018.
Values may be sent and summed in bfloat16 or wider, within the bound.
A program may use at most 128 MiB of HBM per device.

```python
import math
import jax
import jax.numpy as jnp
from jax import lax

CYL = 4
NSF = 256
POL = 2
EWB = 4
NSB = 256
EW_PH = 64
UP = 16
DS = 4
TS = 256
FEEDS = 1024
BEAMS = 1024
CH = 32
TOUT = 4


def draw_voltages(key, part):
    key_base, key_spread = jax.random.split(key, 2)
    chan_index = jnp.arange(CH, dtype=jnp.float32)
    spread = jnp.exp(jax.random.uniform(key_spread, (CH,), dtype=jnp.float32) * jnp.log(10.0))
    rise_curve = 1.0 + 2.0 * chan_index / max(CH - 1, 1)
    noise_part = jnp.clip(jax.random.normal(key_base, (2, FEEDS, POL, CH, TS), dtype=jnp.float32), -4.0, 4.0)
    amplitude = jnp.sqrt(rise_curve * spread)
    return (noise_part * amplitude[None, None, None, :, None]).astype(jnp.bfloat16)


def feed_layout(key):
    return jax.random.permutation(jax.random.fold_in(key, 11), FEEDS).astype(jnp.int32)


def draw_feed_cyl(key, part):
    return (feed_layout(key) // NSF).astype(jnp.int32)


def draw_feed_ns(key, part):
    return (feed_layout(key) % NSF).astype(jnp.int32)


def touch_ends(entries, own_key, least, high):
    longest = entries.shape.index(max(entries.shape))
    spots = []
    for shift in (0, 1):
        where = [jax.random.randint(jax.random.fold_in(own_key, axis), (), 0, length) for axis, length in enumerate(entries.shape)]
        where[longest] = (where[longest] + shift) % entries.shape[longest]
        spots.append(tuple(where))
    return entries.at[spots[0]].set(least).at[spots[1]].set(high)


def levels(rng, extent, shards, smallest, high):
    factor_of = 1.0
    for dim, parts in shards:
        heights = jax.random.uniform(jax.random.fold_in(jax.random.fold_in(rng, 6), dim), (parts,), jnp.float32, smallest / len(shards), high / len(shards))
        factor_of = factor_of * jnp.repeat(jnp.exp(heights), extent[dim] // parts).reshape((-1,) + (1,) * (len(extent) - 1 - dim))
    return factor_of


def setup_inputs(seed: int = 0, part: int = 0) -> dict:
    keys = jax.random.split(jax.random.key(seed), 7)
    own_keys = jax.random.split(jax.random.fold_in(keys[6], part), 7)
    return {
        "voltages": draw_voltages(jax.random.fold_in(jax.random.fold_in(keys[6], part), 71), part),
        "gains": jnp.clip(jax.random.uniform(keys[1], (2, POL, FEEDS), jnp.float32, -1.0, 1.0) * levels(keys[1], (2, POL, FEEDS), ((2, 16),), -0.4, 0.0), -1.0, 1.0),
        "feed_cyl": draw_feed_cyl(jax.random.fold_in(keys[6], 71), part),
        "feed_ns": draw_feed_ns(jax.random.fold_in(keys[6], 71), part),
        "ew_index": touch_ends(jax.random.randint(keys[4], (EWB, CYL), 0, EW_PH), jax.random.fold_in(keys[4], 1), 0, EW_PH - 1).astype(jnp.int32),
        "ns_beam": touch_ends(jax.random.randint(keys[5], (NSB,), 0, 2 * NSF), jax.random.fold_in(keys[5], 1), 0, (2 * NSF) - 1).astype(jnp.int32),
    }


eps_power = 1e-6


def phase_table(feed_cyl, feed_ns, ew_index, ns_beam):
    modulus = 2 * NSF * EW_PH
    cyl_onehot = (feed_cyl[:, None] == jnp.arange(CYL, dtype=jnp.int32)[None, :]).astype(jnp.int32)
    ew_term = jnp.sum(cyl_onehot[:, None, :] * ew_index[None, :, :], axis=2)
    ns_term = feed_ns[:, None] * ns_beam[None, :] * EW_PH
    steps_int = (ew_term[:, :, None] * (2 * NSF) + ns_term[:, None, :]) % modulus
    angles = steps_int.reshape(FEEDS, EWB * NSB).astype(jnp.float32) * (2.0 * math.pi / modulus)
    cosine = jnp.cos(angles).astype(jnp.bfloat16)
    sine_part = jnp.sin(angles).astype(jnp.bfloat16)
    upper_rows = jnp.concatenate([cosine, sine_part], axis=1)
    lower_rows = jnp.concatenate([-sine_part, cosine], axis=1)
    return jnp.concatenate([upper_rows, lower_rows], axis=0)


def upchannel_table():
    bin_index = jnp.arange(UP, dtype=jnp.int32)
    angles = ((bin_index[:, None] * bin_index[None, :]) % UP).astype(jnp.float32) * (2.0 * math.pi / UP)
    cosine = jnp.cos(angles)
    sine_part = jnp.sin(angles)
    return jnp.stack([jnp.stack([cosine, -sine_part], -1), jnp.stack([sine_part, cosine], -1)], 1)


def reference(voltages, gains, feed_cyl, feed_ns, ew_index, ns_beam):
    weights = phase_table(feed_cyl, feed_ns, ew_index, ns_beam)
    fine_table = upchannel_table()
    gain_real = gains[0].T[:, :, None]
    gain_imag = gains[1].T[:, :, None]

    def one_channel(channel):
        sample = lax.dynamic_index_in_dim(voltages, channel, 3, keepdims=False).astype(jnp.float32)
        cal_real = (gain_real * sample[0] - gain_imag * sample[1]).astype(jnp.bfloat16)
        cal_imag = (gain_real * sample[1] + gain_imag * sample[0]).astype(jnp.bfloat16)
        beam_list = []
        for polarity in range(POL):
            stacked = jnp.concatenate([cal_real[:, polarity, :].T, cal_imag[:, polarity, :].T], axis=1)
            beam_list.append(jnp.dot(stacked, weights, preferred_element_type=jnp.float32))
        beam_sums = jnp.stack(beam_list).reshape(POL, TOUT, DS, UP, 2, BEAMS)
        fine_bins = jnp.einsum("pudjrb,jrks->pbudks", beam_sums, fine_table, precision=lax.Precision.HIGHEST)
        return jnp.sum(fine_bins * fine_bins, axis=(0, 3, 5))

    beam_power = lax.map(one_channel, jnp.arange(CH, dtype=jnp.int32))
    beam_power = jnp.transpose(beam_power, (1, 2, 0, 3))
    baseline = jnp.mean(beam_power, axis=(2, 3))
    intensity = beam_power / (baseline[:, :, None, None] + eps_power)
    return intensity.reshape(BEAMS, TOUT, CH * UP)
```

```python
import functools
import math

import jax
import jax.numpy as jnp
from jax import lax
from jax.experimental import pallas as pl
from jax.experimental.pallas import tpu as pltpu
from jax.sharding import PartitionSpec as P

CYL = 4
NSF = 256
EWB = 4
NSB = 256
EW_PH = 64
UP = 16
DS = 4
FEEDS = 1024
BEAMS = 1024
TOUT = 4


eps_power = 1e-06
MESH = pl.DeviceIdType.MESH
PIECES = 4
TWIDDLE = 1.1305
TWIDDLE_GAIN = 1.132804


def phase_table(feed_cyl, feed_ns, ew_index, ns_beam):
    modulus = 2 * NSF * EW_PH
    cyl_onehot = (feed_cyl[:, None] == jnp.arange(CYL, dtype=jnp.int32)[None, :]).astype(jnp.int32)
    ew_term = jnp.sum(cyl_onehot[:, None, :] * ew_index[None, :, :], axis=2)
    ns_term = feed_ns[:, None] * ns_beam[None, :] * EW_PH
    steps_int = (ew_term[:, :, None] * (2 * NSF) + ns_term[:, None, :]) % modulus
    angles = steps_int.reshape(FEEDS, EWB * NSB).astype(jnp.float32) * (2.0 * math.pi / modulus)
    cosine = jnp.cos(angles).astype(jnp.bfloat16)
    sine_part = jnp.sin(angles).astype(jnp.bfloat16)
    upper_rows = jnp.concatenate([cosine, sine_part], axis=1)
    lower_rows = jnp.concatenate([-sine_part, cosine], axis=1)
    return jnp.concatenate([upper_rows, lower_rows], axis=0)


def upchannel_table():
    bin_index = jnp.arange(UP, dtype=jnp.int32)
    angles = (bin_index[:, None] * bin_index[None, :] % UP).astype(jnp.float32) * (
        2.0 * math.pi / UP
    )
    cosine = jnp.cos(angles)
    sine_part = jnp.sin(angles)
    return jnp.stack([jnp.stack([cosine, -sine_part], -1), jnp.stack([sine_part, cosine], -1)], 1)


def shards(voltages, gains, feed_cyl, feed_ns, ew_index, ns_beam):
    weights = phase_table(feed_cyl, feed_ns, ew_index, ns_beam).reshape(2, FEEDS, 2 * BEAMS)
    fine_table = upchannel_table()
    sample = voltages.astype(jnp.float32)
    gain_real = gains[0].T[:, :, None, None]
    gain_imag = gains[1].T[:, :, None, None]
    calibrated = jnp.stack(
        [
            (gain_real * sample[0] - gain_imag * sample[1]).astype(jnp.bfloat16),
            (gain_real * sample[1] + gain_imag * sample[0]).astype(jnp.bfloat16),
        ]
    )
    arrived = lax.all_to_all(calibrated, "chan", split_axis=3, concat_axis=1, tiled=True)
    pieces = arrived.shape[2]
    channels = arrived.shape[3]
    beam_sums = jnp.einsum("rfpct,rfq->pctq", arrived, weights, preferred_element_type=jnp.float32)
    beam_sums = beam_sums.reshape(pieces, channels, TOUT, DS, UP, 2, BEAMS)
    fine_bins = jnp.einsum(
        "pcudjrb,jrks->pbudcks", beam_sums, fine_table, precision=lax.Precision.HIGHEST
    )
    beam_power = jnp.sum(jnp.sum(fine_bins * fine_bins, axis=(3, 6)), axis=0)
    total_chans = beam_power.shape[2] * lax.axis_size("chan")
    band_sum = lax.psum(jnp.sum(beam_power, axis=(2, 3)), "chan")
    baseline = band_sum / (total_chans * UP)
    normed = beam_power / (baseline[:, :, None, None] + eps_power)
    intensity = lax.all_to_all(normed, "chan", split_axis=0, concat_axis=2, tiled=True)
    return intensity.reshape(intensity.shape[0], TOUT, intensity.shape[2] * UP)


def cos_sin(steps):
    quarter = (steps + 64) >> 7
    x = (steps - (quarter << 7)).astype(jnp.float32) * (2.0 * math.pi / 512)
    y = x * x
    s = x * (1.0 + y * (-1 / 6 + y * (1 / 120 + y * (-1 / 5040 + y * (1 / 362880)))))
    c = 1.0 + y * (-0.5 + y * (1 / 24 + y * (-1 / 720 + y * (1 / 40320))))
    odd = (quarter & 1) == 1
    cosine = jnp.where(odd, s, c)
    sine = jnp.where(odd, c, s)
    cosine = jnp.where(((quarter + 1) & 2) == 2, -cosine, cosine)
    sine = jnp.where((quarter & 2) == 2, -sine, sine)
    return cosine, sine


def encode(power):
    small = power < 2.0**-17
    scaled = jnp.where(small, power * -(2.0**80), power * 2.0**17)
    return (scaled * jnp.abs(scaled)).astype(jnp.bfloat16)


def decode(code):
    code = code.astype(jnp.float32)
    size = jnp.abs(code)
    root = size * lax.rsqrt(jnp.maximum(size, 2.0**-126))
    return root * jnp.where(code < 0, 2.0**-80, 2.0**-17)


def flip(me, m):
    bits = [lax.rem(me // b + m // b, 2) * b for b in (1, 2, 4, 8)]
    return bits[0] + bits[1] + bits[2] + bits[3]


def beam_kernel(
    n, volt_ref, gain_ref, cyl_ref, ns_ref, ew_ref, nb_ref, out_ref,
    volt, wide, gcol, ncol, dft, xin, x_ref,
    recv, wre, wim, sums, pbuf, precv,
    volt_sem, send_sem, recv_sem, own_sem, psend_sem, precv_sem, pown_sem,
):
    me = lax.axis_index("chan")

    def fetch(i):
        feeds = pl.ds(pl.multiple_of(i * 8, 8), 8)
        return pltpu.make_async_copy(volt_ref.at[:, feeds], volt.at[:, feeds], volt_sem.at[i])

    def begin(i, carry):
        fetch(i).start()
        return carry

    lax.fori_loop(0, 8, begin, 0)
    barrier = pltpu.get_barrier_semaphore()

    def greet(s, carry):
        pl.semaphore_signal(
            barrier, inc=1, device_id={"chan": lax.rem(me + s, n)}, device_id_type=MESH
        )
        return carry

    lax.fori_loop(1, n, greet, 0)

    row = lax.broadcasted_iota(jnp.int32, dft.shape, 0)
    col = lax.broadcasted_iota(jnp.int32, dft.shape, 1)
    same = (((row >> 6) & 1) == ((col >> 4) & 1)) & (((row >> 4) & 3) == ((col >> 5) & 3))
    turns = (row & 15) * (col & 15) * 32 + ((col >> 7) - (row >> 7)) * 128
    dft[...] = jnp.where(same, cos_sin(turns & 511)[0] * TWIDDLE, 0.0).astype(jnp.bfloat16)
    for r in range(2):
        for p in range(2):
            gcol[r, p] = jnp.broadcast_to(gain_ref[r, p : p + 1, :], (128, 64)).T

    def widen(i, carry):
        fetch(i).wait()
        first = pl.multiple_of(i * 8 * 2 * n, 8 * 2 * n)
        for r in range(2):
            for p in range(2):
                part = volt[r, pl.ds(pl.multiple_of(i * 8, 8), 8), p].astype(jnp.float32)
                part = part.reshape(8 * 2 * n, 256)
                for h in range(2):
                    wide[r, p, h, pl.ds(first, 8 * 2 * n), :] = part[:, h * 128 : (h + 1) * 128]
        return carry

    lax.fori_loop(0, 8, widen, 0)
    pl.semaphore_wait(barrier, n - 1)

    def volt_copy(q, m):
        d = flip(me, m)
        return pltpu.make_async_remote_copy(
            src_ref=x_ref.at[d, q],
            dst_ref=recv.at[q, me // 2, :, lax.rem(me, 2)],
            send_sem=send_sem.at[q, m],
            recv_sem=recv_sem.at[q, m],
            device_id={"chan": d},
            device_id_type=MESH,
        )

    def own_copy(q):
        return pltpu.make_async_copy(
            x_ref.at[me, q], recv.at[q, me // 2, :, lax.rem(me, 2)], own_sem.at[q]
        )

    def power_copy(q, m):
        d = flip(me, m)
        return pltpu.make_async_remote_copy(
            src_ref=pbuf.at[q, d],
            dst_ref=precv.at[q, me],
            send_sem=psend_sem.at[q, m],
            recv_sem=precv_sem.at[q, m],
            device_id={"chan": d},
            device_id_type=MESH,
        )

    def own_power(q):
        return pltpu.make_async_copy(pbuf.at[q, me], precv.at[q, me], pown_sem.at[q])

    def partner(i):
        return lax.rem(i, 2) * lax.rem((i + 1) // 2, 8) + (1 - lax.rem(i, 2)) * (8 + i // 2)

    def each(make, act, q):
        def one(i, carry):
            getattr(make(q, partner(i)), act)()
            return carry

        lax.fori_loop(0, n - 1, one, 0)

    def produce(i, carry):
        m = partner(i)
        d = flip(me, m)
        for p in range(2):
            gr = gcol[0, p]
            gi = gcol[1, p]
            for c in range(2):
                for h in range(2):
                    at = pl.ds(d * 2 + c, 64, stride=2 * n)
                    real = wide[0, p, h, at, :]
                    imag = wide[1, p, h, at, :]
                    first = ((h * 2 + c) * 2 + p) * 64
                    xin[first : first + 64, :128] = (gr * real - gi * imag).astype(jnp.bfloat16)
                    xin[first : first + 64, 128:] = (gr * imag + gi * real).astype(jnp.bfloat16)
        bins = jnp.dot(xin[...], dft[...], preferred_element_type=jnp.float32)
        for q in range(PIECES):
            for p in range(2):
                part = bins[(q * 2 + p) * 64 : (q * 2 + p) * 64 + 64].astype(jnp.bfloat16)
                for r in range(2):
                    x_ref[d, q, r, :, p * 128 : (p + 1) * 128] = part[:, r * 128 : (r + 1) * 128]

        @pl.when(i < n - 1)
        def _():
            volt_copy(0, m).start()

        return carry

    lax.fori_loop(0, n, produce, 0)
    for q in range(1, PIECES):
        each(volt_copy, "start", q)
    for q in range(PIECES):
        own_copy(q).start()

    for h in range(2):
        ncol[h * 128 : (h + 1) * 128, :] = jnp.broadcast_to(nb_ref[h : h + 1, :], (128, 128)).T

    def table(i, carry):
        real = pl.ds(pl.multiple_of(i * 256, 256), 128)
        imag = pl.ds(pl.multiple_of(i * 256 + 128, 128), 128)
        cyl = cyl_ref[pl.ds(i, 1), :]
        ns = jnp.broadcast_to(ns_ref[pl.ds(i, 1), :], (128, 128))
        for h in range(2):
            slope = ns * ncol[h * 128 : (h + 1) * 128, :]
            for e in range(EWB):
                shift = jnp.where(
                    cyl < 2,
                    jnp.where(cyl == 0, ew_ref[e, 0], ew_ref[e, 1]),
                    jnp.where(cyl == 2, ew_ref[e, 2], ew_ref[e, 3]),
                )
                cosine, sine = cos_sin((slope + shift * 8) & 511)
                rows = slice(e * NSB + h * 128, e * NSB + h * 128 + 128)
                cosine = cosine.astype(jnp.bfloat16)
                wre[rows, real] = cosine
                wim[rows, imag] = cosine
                wim[rows, real] = sine.astype(jnp.bfloat16)
                wre[rows, imag] = (-sine).astype(jnp.bfloat16)
        return carry

    lax.fori_loop(0, FEEDS // 128, table, 0)
    blocks = BEAMS // 256
    lane = lax.broadcasted_iota(jnp.int32, (16, 128), 1)
    on = {w: (lane & w) != 0 for w in (16, 32, 64)}

    for q in range(PIECES):
        each(volt_copy, "wait_recv", q)
        own_copy(q).wait()

        def block(i, carry, q=q):
            nb = lax.rem(i + (1 - me // 8) * 2, blocks)
            rows = pl.ds(pl.multiple_of(nb * 256, 256), 256)
            feeds = recv[q].reshape(2 * FEEDS, 256)
            sums[0] = jnp.dot(wre[rows, :], feeds, preferred_element_type=jnp.float32)
            sums[1] = jnp.dot(wim[rows, :], feeds, preferred_element_type=jnp.float32)
            for o in range(4):
                parts = []
                for g in range(4):
                    at = slice(o * 64 + g * 16, o * 64 + g * 16 + 16)
                    real = sums[0, at, :]
                    imag = sums[1, at, :]
                    power = real * real + imag * imag
                    parts.append(power[:, :128] + power[:, 128:])
                halves = [
                    jnp.where(on[64], b, a) + pltpu.roll(jnp.where(on[64], a, b), 64, 1)
                    for a, b in ((parts[0], parts[2]), (parts[1], parts[3]))
                ]
                other = jnp.where(on[32], halves[0], halves[1])
                total = jnp.where(on[32], halves[1], halves[0]) + jnp.where(
                    on[32], pltpu.roll(other, 32, 1), pltpu.roll(other, 96, 1)
                )
                pbuf[q, nb * 4 + o] = encode(total)
            for o in range(4):
                m = flip(me, nb * 4 + o)

                @pl.when(m > 0)
                def _(m=m):
                    power_copy(q, m).start()

            return carry

        lax.fori_loop(0, blocks, block, 0)
        own_power(q).start()

    for q in range(PIECES):
        each(volt_copy, "wait_send", q)

    for h in range(2):
        for c in range(2):
            each(power_copy, "wait_recv", h * 2 + c)
            own_power(h * 2 + c).wait()
        tiles = []
        for t in range(4):
            vals = [
                decode(precv[h * 2 + c, 4 * t + s]) for s in range(4) for c in range(2)
            ]
            for b in range(3):
                w = 16 << b
                for a in range(8):
                    if not a >> b & 1:
                        z = a | 1 << b
                        vals[a], vals[z] = (
                            jnp.where(on[w], pltpu.roll(vals[z], w, 1), vals[a]),
                            jnp.where(on[w], vals[z], pltpu.roll(vals[a], 128 - w, 1)),
                        )
            tiles.append(vals)
        for a in range(8):
            total = tiles[0][a] + tiles[1][a] + tiles[2][a] + tiles[3][a]
            baseline = jnp.sum(total, axis=1, keepdims=True) * (1.0 / (n * 32))
            scale = 1.0 / (baseline + eps_power * TWIDDLE_GAIN**2)
            for t in range(4):
                at = (a >> 1) * 256 + t * 4 + h * 2 + (a & 1)
                out_ref[pl.ds(at, 16, stride=16), :] = tiles[t][a] * scale
    for q in range(PIECES):
        each(power_copy, "wait_send", q)


def fused(n, voltages, gains, feed_cyl, feed_ns, ew_index, ns_beam):
    vmem = pl.BlockSpec(memory_space=pltpu.VMEM)
    dma = pltpu.SemaphoreType.DMA
    out = pl.pallas_call(
        functools.partial(beam_kernel, n),
        out_shape=jax.ShapeDtypeStruct((1024, 128), jnp.float32),
        in_specs=[
            pl.BlockSpec(memory_space=pl.ANY), vmem, vmem, vmem,
            pl.BlockSpec(memory_space=pltpu.SMEM), vmem,
        ],
        out_specs=vmem,
        scratch_shapes=[
            pltpu.VMEM(voltages.shape, jnp.bfloat16),
            pltpu.VMEM((2, 2, 2, 64 * 2 * n, 128), jnp.float32),
            pltpu.VMEM((2, 2, 64, 128), jnp.float32),
            pltpu.VMEM((NSB, 128), jnp.int32),
            pltpu.VMEM((256, 256), jnp.bfloat16),
            pltpu.VMEM((512, 256), jnp.bfloat16),
            pltpu.VMEM((n, PIECES, 2, 64, 256), jnp.bfloat16),
            pltpu.VMEM((PIECES, n // 2, 2, 2, 64, 256), jnp.bfloat16),
            pltpu.VMEM((BEAMS, 2 * FEEDS), jnp.bfloat16),
            pltpu.VMEM((BEAMS, 2 * FEEDS), jnp.bfloat16),
            pltpu.VMEM((2, 256, 256), jnp.float32),
            pltpu.VMEM((PIECES, n, 16, 128), jnp.bfloat16),
            pltpu.VMEM((PIECES, n, 16, 128), jnp.bfloat16),
            dma((8,)), dma((PIECES, n)), dma((PIECES, n)), dma((PIECES,)),
            dma((PIECES, n)), dma((PIECES, n)), dma((PIECES,)),
        ],
        compiler_params=pltpu.CompilerParams(
            collective_id=0, has_side_effects=True, vmem_limit_bytes=56 << 20
        ),
    )(
        voltages, gains, feed_cyl.reshape(-1, 128), feed_ns.reshape(-1, 128),
        ew_index, ns_beam.reshape(-1, 128),
    )
    return out.reshape(64, 4, TOUT, 128).transpose(0, 2, 1, 3).reshape(64, TOUT, 512)


def solution(mesh):
    placed = (P(None, "chan", None, None, "grp"), P(None, None, "chan"), P(), P(), P(), P())
    n = mesh.shape["chan"]

    def part(voltages, gains, feed_cyl, feed_ns, ew_index, ns_beam):
        fits = voltages.shape == (2, 64, 2, 2 * n, UP * DS * TOUT) and n * 64 == FEEDS
        run = functools.partial(fused, n) if fits else shards
        return run(voltages, gains, feed_cyl, feed_ns, ew_index, ns_beam)

    return jax.shard_map(
        part, mesh=mesh, in_specs=placed, out_specs=P("chan", "grp", None), check_vma=False
    )
```

```python
import functools
import math

import jax
import jax.numpy as jnp
from jax import lax
from jax.experimental import pallas as pl
from jax.experimental.pallas import tpu as pltpu
from jax.sharding import PartitionSpec as P

CYL = 4
NSF = 256
EWB = 4
NSB = 256
EW_PH = 64
UP = 16
DS = 4
FEEDS = 1024
BEAMS = 1024
TOUT = 4


eps_power = 1e-06
MESH = pl.DeviceIdType.MESH
PIECES = 4
GROUPS = ((0, 3), (3, 1))
ORDER = (8, 1, 9, 2, 10, 3, 11, 4, 12, 5, 13, 6, 14, 7, 15)
TWIDDLE = 1.1305
TWIDDLE_GAIN = 1.132804


def phase_table(feed_cyl, feed_ns, ew_index, ns_beam):
    modulus = 2 * NSF * EW_PH
    cyl_onehot = (feed_cyl[:, None] == jnp.arange(CYL, dtype=jnp.int32)[None, :]).astype(jnp.int32)
    ew_term = jnp.sum(cyl_onehot[:, None, :] * ew_index[None, :, :], axis=2)
    ns_term = feed_ns[:, None] * ns_beam[None, :] * EW_PH
    steps_int = (ew_term[:, :, None] * (2 * NSF) + ns_term[:, None, :]) % modulus
    angles = steps_int.reshape(FEEDS, EWB * NSB).astype(jnp.float32) * (2.0 * math.pi / modulus)
    cosine = jnp.cos(angles).astype(jnp.bfloat16)
    sine_part = jnp.sin(angles).astype(jnp.bfloat16)
    upper_rows = jnp.concatenate([cosine, sine_part], axis=1)
    lower_rows = jnp.concatenate([-sine_part, cosine], axis=1)
    return jnp.concatenate([upper_rows, lower_rows], axis=0)


def upchannel_table():
    bin_index = jnp.arange(UP, dtype=jnp.int32)
    angles = (bin_index[:, None] * bin_index[None, :] % UP).astype(jnp.float32) * (
        2.0 * math.pi / UP
    )
    cosine = jnp.cos(angles)
    sine_part = jnp.sin(angles)
    return jnp.stack([jnp.stack([cosine, -sine_part], -1), jnp.stack([sine_part, cosine], -1)], 1)


def shards(voltages, gains, feed_cyl, feed_ns, ew_index, ns_beam):
    weights = phase_table(feed_cyl, feed_ns, ew_index, ns_beam).reshape(2, FEEDS, 2 * BEAMS)
    fine_table = upchannel_table()
    sample = voltages.astype(jnp.float32)
    gain_real = gains[0].T[:, :, None, None]
    gain_imag = gains[1].T[:, :, None, None]
    calibrated = jnp.stack(
        [
            (gain_real * sample[0] - gain_imag * sample[1]).astype(jnp.bfloat16),
            (gain_real * sample[1] + gain_imag * sample[0]).astype(jnp.bfloat16),
        ]
    )
    arrived = lax.all_to_all(calibrated, "chan", split_axis=3, concat_axis=1, tiled=True)
    pieces = arrived.shape[2]
    channels = arrived.shape[3]
    beam_sums = jnp.einsum("rfpct,rfq->pctq", arrived, weights, preferred_element_type=jnp.float32)
    beam_sums = beam_sums.reshape(pieces, channels, TOUT, DS, UP, 2, BEAMS)
    fine_bins = jnp.einsum(
        "pcudjrb,jrks->pbudcks", beam_sums, fine_table, precision=lax.Precision.HIGHEST
    )
    beam_power = jnp.sum(jnp.sum(fine_bins * fine_bins, axis=(3, 6)), axis=0)
    total_chans = beam_power.shape[2] * lax.axis_size("chan")
    band_sum = lax.psum(jnp.sum(beam_power, axis=(2, 3)), "chan")
    baseline = band_sum / (total_chans * UP)
    normed = beam_power / (baseline[:, :, None, None] + eps_power)
    intensity = lax.all_to_all(normed, "chan", split_axis=0, concat_axis=2, tiled=True)
    return intensity.reshape(intensity.shape[0], TOUT, intensity.shape[2] * UP)


def cos_sin(steps):
    quarter = (steps + 64) >> 7
    x = (steps - (quarter << 7)).astype(jnp.float32) * (2.0 * math.pi / 512)
    y = x * x
    s = x * (1.0 + y * (-1 / 6 + y * (1 / 120 + y * (-1 / 5040 + y * (1 / 362880)))))
    c = 1.0 + y * (-0.5 + y * (1 / 24 + y * (-1 / 720 + y * (1 / 40320))))
    odd = (quarter & 1) == 1
    cosine = jnp.where(odd, s, c)
    sine = jnp.where(odd, c, s)
    cosine = jnp.where(((quarter + 1) & 2) == 2, -cosine, cosine)
    sine = jnp.where((quarter & 2) == 2, -sine, sine)
    return cosine, sine


def encode(power):
    small = power < 2.0**-17
    scaled = jnp.where(small, power * -(2.0**80), power * 2.0**17)
    return (scaled * jnp.abs(scaled)).astype(jnp.bfloat16)


def decode(code):
    code = code.astype(jnp.float32)
    size = jnp.abs(code)
    root = size * lax.rsqrt(jnp.maximum(size, 2.0**-126))
    return root * jnp.where(code < 0, 2.0**-80, 2.0**-17)


def flip(me, m):
    bits = [lax.rem(me // b + m // b, 2) * b for b in (1, 2, 4, 8)]
    return bits[0] + bits[1] + bits[2] + bits[3]


def beam_kernel(
    n, volt_ref, gain_ref, cyl_ref, ns_ref, ew_ref, nb_ref, out_ref,
    volt, wide, gcol, ncol, dft, xin, x_ref,
    recv, wre, wim, sums, pbuf, precv,
    volt_sem, send_sem, recv_sem, own_sem, psend_sem, precv_sem, pown_sem,
):
    me = lax.axis_index("chan")

    def fetch(i):
        feeds = pl.ds(pl.multiple_of(i * 8, 8), 8)
        return pltpu.make_async_copy(volt_ref.at[:, feeds], volt.at[:, feeds], volt_sem.at[i])

    def begin(i, carry):
        fetch(i).start()
        return carry

    lax.fori_loop(0, 8, begin, 0)
    barrier = pltpu.get_barrier_semaphore()

    def greet(s, carry):
        pl.semaphore_signal(
            barrier, inc=1, device_id={"chan": lax.rem(me + s, n)}, device_id_type=MESH
        )
        return carry

    lax.fori_loop(1, n, greet, 0)

    row = lax.broadcasted_iota(jnp.int32, dft.shape, 0)
    col = lax.broadcasted_iota(jnp.int32, dft.shape, 1)
    same = (((row >> 6) & 1) == ((col >> 4) & 1)) & (((row >> 4) & 3) == ((col >> 5) & 3))
    turns = (row & 15) * (col & 15) * 32 + ((col >> 7) - (row >> 7)) * 128
    dft[...] = jnp.where(same, cos_sin(turns & 511)[0] * TWIDDLE, 0.0).astype(jnp.bfloat16)
    for r in range(2):
        for p in range(2):
            gcol[r, p] = jnp.broadcast_to(gain_ref[r, p : p + 1, :], (128, 64)).T

    def widen(i, carry):
        fetch(i).wait()
        first = pl.multiple_of(i * 8 * 2 * n, 8 * 2 * n)
        for r in range(2):
            for p in range(2):
                part = volt[r, pl.ds(pl.multiple_of(i * 8, 8), 8), p].astype(jnp.float32)
                part = part.reshape(8 * 2 * n, 256)
                for h in range(2):
                    wide[r, p, h, pl.ds(first, 8 * 2 * n), :] = part[:, h * 128 : (h + 1) * 128]
        return carry

    lax.fori_loop(0, 8, widen, 0)
    pl.semaphore_wait(barrier, n - 1)

    def volt_copy(g, m):
        d = flip(me, m)
        return pltpu.make_async_remote_copy(
            src_ref=x_ref.at[d, pl.ds(*GROUPS[g])],
            dst_ref=recv.at[pl.ds(*GROUPS[g]), me // 2, :, lax.rem(me, 2)],
            send_sem=send_sem.at[g, m],
            recv_sem=recv_sem.at[g, m],
            device_id={"chan": d},
            device_id_type=MESH,
        )

    def own_copy(g):
        return pltpu.make_async_copy(
            x_ref.at[me, pl.ds(*GROUPS[g])],
            recv.at[pl.ds(*GROUPS[g]), me // 2, :, lax.rem(me, 2)],
            own_sem.at[g],
        )

    def power_copy(g, m):
        d = flip(me, m)
        return pltpu.make_async_remote_copy(
            src_ref=pbuf.at[d, pl.ds(*GROUPS[g])],
            dst_ref=precv.at[me, pl.ds(*GROUPS[g])],
            send_sem=psend_sem.at[g, m],
            recv_sem=precv_sem.at[g, m],
            device_id={"chan": d},
            device_id_type=MESH,
        )

    def own_power(g):
        return pltpu.make_async_copy(
            pbuf.at[me, pl.ds(*GROUPS[g])], precv.at[me, pl.ds(*GROUPS[g])], pown_sem.at[g]
        )

    def partner(i):
        return lax.rem(i, 2) * lax.rem((i + 1) // 2, 8) + (1 - lax.rem(i, 2)) * (8 + i // 2)

    def each(make, act, g, partners=ORDER):
        for m in partners:
            getattr(make(g, m), act)()

    def produce(i, carry):
        m = partner(i)
        d = flip(me, m)
        for p in range(2):
            gr = gcol[0, p]
            gi = gcol[1, p]
            for c in range(2):
                for h in range(2):
                    at = pl.ds(d * 2 + c, 64, stride=2 * n)
                    real = wide[0, p, h, at, :]
                    imag = wide[1, p, h, at, :]
                    first = ((h * 2 + c) * 2 + p) * 64
                    xin[first : first + 64, :128] = (gr * real - gi * imag).astype(jnp.bfloat16)
                    xin[first : first + 64, 128:] = (gr * imag + gi * real).astype(jnp.bfloat16)
        bins = jnp.dot(xin[...], dft[...], preferred_element_type=jnp.float32)
        for q in range(PIECES):
            for p in range(2):
                part = bins[(q * 2 + p) * 64 : (q * 2 + p) * 64 + 64].astype(jnp.bfloat16)
                for r in range(2):
                    x_ref[d, q, r, :, p * 128 : (p + 1) * 128] = part[:, r * 128 : (r + 1) * 128]

        @pl.when(i < n - 1)
        def _():
            volt_copy(0, m).start()

        return carry

    lax.fori_loop(0, n, produce, 0)
    for g in range(2):
        own_copy(g).start()

    for h in range(2):
        ncol[h * 128 : (h + 1) * 128, :] = jnp.broadcast_to(nb_ref[h : h + 1, :], (128, 128)).T

    def table(i, carry):
        real = pl.ds(pl.multiple_of(i * 256, 256), 128)
        imag = pl.ds(pl.multiple_of(i * 256 + 128, 128), 128)
        cyl = cyl_ref[pl.ds(i, 1), :]
        ns = jnp.broadcast_to(ns_ref[pl.ds(i, 1), :], (128, 128))
        for h in range(2):
            slope = ns * ncol[h * 128 : (h + 1) * 128, :]
            for e in range(EWB):
                shift = jnp.where(
                    cyl < 2,
                    jnp.where(cyl == 0, ew_ref[e, 0], ew_ref[e, 1]),
                    jnp.where(cyl == 2, ew_ref[e, 2], ew_ref[e, 3]),
                )
                cosine, sine = cos_sin((slope + shift * 8) & 511)
                rows = slice(e * NSB + h * 128, e * NSB + h * 128 + 128)
                cosine = cosine.astype(jnp.bfloat16)
                wre[rows, real] = cosine
                wim[rows, imag] = cosine
                wim[rows, real] = sine.astype(jnp.bfloat16)
                wre[rows, imag] = (-sine).astype(jnp.bfloat16)
        return carry

    lax.fori_loop(0, FEEDS // 128, table, 0)
    blocks = BEAMS // 256
    lane = lax.broadcasted_iota(jnp.int32, (16, 128), 1)
    on = {w: (lane & w) != 0 for w in (16, 32, 64)}


    def finish(q, nb):
        for o in range(4):
            parts = []
            for g in range(4):
                at = pl.ds(pl.multiple_of(nb * 256 + o * 64 + g * 16, 16), 16)
                real = sums[q, 0, at, :]
                imag = sums[q, 1, at, :]
                power = real * real + imag * imag
                parts.append(power[:, :128] + power[:, 128:])
            halves = [
                jnp.where(on[64], b, a) + pltpu.roll(jnp.where(on[64], a, b), 64, 1)
                for a, b in ((parts[0], parts[2]), (parts[1], parts[3]))
            ]
            other = jnp.where(on[32], halves[0], halves[1])
            total = jnp.where(on[32], halves[1], halves[0]) + jnp.where(
                on[32], pltpu.roll(other, 32, 1), pltpu.roll(other, 96, 1)
            )
            pbuf[nb * 4 + o, q] = encode(total)

    def add(q, nb, first, tiles, fresh):
        rows = pl.ds(pl.multiple_of(nb * 256, 256), 256)
        terms = pl.ds(pl.multiple_of(first * 256, 256), tiles * 256)
        feeds = recv[q, pl.ds(first, tiles)].reshape(tiles * 256, 256)
        for r, weights in enumerate((wre, wim)):
            part = jnp.dot(weights[rows, terms], feeds, preferred_element_type=jnp.float32)
            sums[q, r, rows, :] = part if fresh else sums[q, r, rows, :] + part

    def beams(body):
        def one(i, carry):
            body(lax.rem(i + (1 - me // 8) * 2, blocks))
            return carry

        lax.fori_loop(0, blocks, one, 0)

    each(volt_copy, "start", 1)
    near = me // 8 * 4
    far = (flip(me, 8) // 4 * 2, flip(me, 12) // 4 * 2)
    for g in range(2):
        own_copy(g).wait()
        each(volt_copy, "wait_recv", g, range(1, 8))
        for q in range(GROUPS[g][0], sum(GROUPS[g])):
            beams(lambda nb, q=q: add(q, nb, near, 4, True))
    each(volt_copy, "wait_recv", 0, range(8, 12))
    for q in range(3):
        beams(lambda nb, q=q: add(q, nb, far[0], 2, False))
    each(volt_copy, "wait_recv", 0, range(12, 16))
    for q in range(3):

        def whole(nb, q=q):
            add(q, nb, far[1], 2, False)
            finish(q, nb)

        beams(whole)
    each(power_copy, "start", 0)
    own_power(0).start()
    each(volt_copy, "wait_recv", 1, range(8, 12))
    beams(lambda nb: add(3, nb, far[0], 2, False))
    each(volt_copy, "wait_recv", 1, range(12, 16))

    def last(nb):
        add(3, nb, far[1], 2, False)
        finish(3, nb)
        for o in range(4):
            m = flip(me, nb * 4 + o)

            @pl.when(m > 0)
            def _(m=m):
                power_copy(1, m).start()

    beams(last)
    own_power(1).start()
    each(volt_copy, "wait_send", 0)
    each(volt_copy, "wait_send", 1)

    for h in range(2):
        each(power_copy, "wait_recv", h)
        own_power(h).wait()
        tiles = []
        for t in range(4):
            vals = [
                decode(precv[4 * t + s, h * 2 + c]) for s in range(4) for c in range(2)
            ]
            for b in range(3):
                w = 16 << b
                for a in range(8):
                    if not a >> b & 1:
                        z = a | 1 << b
                        vals[a], vals[z] = (
                            jnp.where(on[w], pltpu.roll(vals[z], w, 1), vals[a]),
                            jnp.where(on[w], vals[z], pltpu.roll(vals[a], 128 - w, 1)),
                        )
            tiles.append(vals)
        for a in range(8):
            total = tiles[0][a] + tiles[1][a] + tiles[2][a] + tiles[3][a]
            baseline = jnp.sum(total, axis=1, keepdims=True) * (1.0 / (n * 32))
            scale = 1.0 / (baseline + eps_power * TWIDDLE_GAIN**2)
            for t in range(4):
                at = (a >> 1) * 256 + t * 4 + h * 2 + (a & 1)
                out_ref[pl.ds(at, 16, stride=16), :] = tiles[t][a] * scale
    for g in range(2):
        each(power_copy, "wait_send", g)


def fused(n, voltages, gains, feed_cyl, feed_ns, ew_index, ns_beam):
    vmem = pl.BlockSpec(memory_space=pltpu.VMEM)
    dma = pltpu.SemaphoreType.DMA
    out = pl.pallas_call(
        functools.partial(beam_kernel, n),
        out_shape=pltpu.VMEM((1024, 128), jnp.float32),
        in_specs=[
            pl.BlockSpec(memory_space=pl.ANY), vmem, vmem, vmem,
            pl.BlockSpec(memory_space=pltpu.SMEM), vmem,
        ],
        out_specs=vmem,
        scratch_shapes=[
            pltpu.VMEM(voltages.shape, jnp.bfloat16),
            pltpu.VMEM((2, 2, 2, 64 * 2 * n, 128), jnp.float32),
            pltpu.VMEM((2, 2, 64, 128), jnp.float32),
            pltpu.VMEM((NSB, 128), jnp.int32),
            pltpu.VMEM((256, 256), jnp.bfloat16),
            pltpu.VMEM((512, 256), jnp.bfloat16),
            pltpu.VMEM((n, PIECES, 2, 64, 256), jnp.bfloat16),
            pltpu.VMEM((PIECES, n // 2, 2, 2, 64, 256), jnp.bfloat16),
            pltpu.VMEM((BEAMS, 2 * FEEDS), jnp.bfloat16),
            pltpu.VMEM((BEAMS, 2 * FEEDS), jnp.bfloat16),
            pltpu.VMEM((PIECES, 2, BEAMS, 256), jnp.float32),
            pltpu.VMEM((n, PIECES, 16, 128), jnp.bfloat16),
            pltpu.VMEM((n, PIECES, 16, 128), jnp.bfloat16),
            dma((8,)), dma((2, n)), dma((2, n)), dma((2,)),
            dma((2, n)), dma((2, n)), dma((2,)),
        ],
        compiler_params=pltpu.CompilerParams(
            collective_id=0, has_side_effects=True, vmem_limit_bytes=56 << 20
        ),
    )(
        voltages, gains, feed_cyl.reshape(-1, 128), feed_ns.reshape(-1, 128),
        ew_index, ns_beam.reshape(-1, 128),
    )
    return out.reshape(64, 4, TOUT, 128).transpose(0, 2, 1, 3).reshape(64, TOUT, 512)


def solution(mesh):
    placed = (P(None, "chan", None, None, "grp"), P(None, None, "chan"), P(), P(), P(), P())
    n = mesh.shape["chan"]

    def part(voltages, gains, feed_cyl, feed_ns, ew_index, ns_beam):
        fits = voltages.shape == (2, 64, 2, 2 * n, UP * DS * TOUT) and n * 64 == FEEDS
        run = functools.partial(fused, n) if fits else shards
        return run(voltages, gains, feed_cyl, feed_ns, ew_index, ns_beam)

    return jax.shard_map(
        part, mesh=mesh, in_specs=placed, out_specs=P("chan", "grp", None), check_vma=False
    )
```

```python
import functools
import math

import jax
import jax.numpy as jnp
from jax import lax
from jax.experimental import pallas as pl
from jax.experimental.pallas import tpu as pltpu
from jax.sharding import PartitionSpec as P

CYL = 4
NSF = 256
EWB = 4
NSB = 256
EW_PH = 64
UP = 16
DS = 4
FEEDS = 1024
BEAMS = 1024
TOUT = 4


eps_power = 1e-06
MESH = pl.DeviceIdType.MESH
PIECES = 4
EARLY = 1
GROUPS = ((0, 3), (3, 1))
ORDER = (8, 1, 9, 2, 10, 3, 11, 4, 12, 5, 13, 6, 14, 7, 15)
TWIDDLE = 1.1305
TWIDDLE_GAIN = 1.132804


def phase_table(feed_cyl, feed_ns, ew_index, ns_beam):
    modulus = 2 * NSF * EW_PH
    cyl_onehot = (feed_cyl[:, None] == jnp.arange(CYL, dtype=jnp.int32)[None, :]).astype(jnp.int32)
    ew_term = jnp.sum(cyl_onehot[:, None, :] * ew_index[None, :, :], axis=2)
    ns_term = feed_ns[:, None] * ns_beam[None, :] * EW_PH
    steps_int = (ew_term[:, :, None] * (2 * NSF) + ns_term[:, None, :]) % modulus
    angles = steps_int.reshape(FEEDS, EWB * NSB).astype(jnp.float32) * (2.0 * math.pi / modulus)
    cosine = jnp.cos(angles).astype(jnp.bfloat16)
    sine_part = jnp.sin(angles).astype(jnp.bfloat16)
    upper_rows = jnp.concatenate([cosine, sine_part], axis=1)
    lower_rows = jnp.concatenate([-sine_part, cosine], axis=1)
    return jnp.concatenate([upper_rows, lower_rows], axis=0)


def upchannel_table():
    bin_index = jnp.arange(UP, dtype=jnp.int32)
    angles = (bin_index[:, None] * bin_index[None, :] % UP).astype(jnp.float32) * (
        2.0 * math.pi / UP
    )
    cosine = jnp.cos(angles)
    sine_part = jnp.sin(angles)
    return jnp.stack([jnp.stack([cosine, -sine_part], -1), jnp.stack([sine_part, cosine], -1)], 1)


def shards(voltages, gains, feed_cyl, feed_ns, ew_index, ns_beam):
    weights = phase_table(feed_cyl, feed_ns, ew_index, ns_beam).reshape(2, FEEDS, 2 * BEAMS)
    fine_table = upchannel_table()
    sample = voltages.astype(jnp.float32)
    gain_real = gains[0].T[:, :, None, None]
    gain_imag = gains[1].T[:, :, None, None]
    calibrated = jnp.stack(
        [
            (gain_real * sample[0] - gain_imag * sample[1]).astype(jnp.bfloat16),
            (gain_real * sample[1] + gain_imag * sample[0]).astype(jnp.bfloat16),
        ]
    )
    arrived = lax.all_to_all(calibrated, "chan", split_axis=3, concat_axis=1, tiled=True)
    pieces = arrived.shape[2]
    channels = arrived.shape[3]
    beam_sums = jnp.einsum("rfpct,rfq->pctq", arrived, weights, preferred_element_type=jnp.float32)
    beam_sums = beam_sums.reshape(pieces, channels, TOUT, DS, UP, 2, BEAMS)
    fine_bins = jnp.einsum(
        "pcudjrb,jrks->pbudcks", beam_sums, fine_table, precision=lax.Precision.HIGHEST
    )
    beam_power = jnp.sum(jnp.sum(fine_bins * fine_bins, axis=(3, 6)), axis=0)
    total_chans = beam_power.shape[2] * lax.axis_size("chan")
    band_sum = lax.psum(jnp.sum(beam_power, axis=(2, 3)), "chan")
    baseline = band_sum / (total_chans * UP)
    normed = beam_power / (baseline[:, :, None, None] + eps_power)
    intensity = lax.all_to_all(normed, "chan", split_axis=0, concat_axis=2, tiled=True)
    return intensity.reshape(intensity.shape[0], TOUT, intensity.shape[2] * UP)


def cos_sin(steps):
    quarter = (steps + 64) >> 7
    x = (steps - (quarter << 7)).astype(jnp.float32) * (2.0 * math.pi / 512)
    y = x * x
    s = x * (1.0 + y * (-1 / 6 + y * (1 / 120 + y * (-1 / 5040 + y * (1 / 362880)))))
    c = 1.0 + y * (-0.5 + y * (1 / 24 + y * (-1 / 720 + y * (1 / 40320))))
    odd = (quarter & 1) == 1
    cosine = jnp.where(odd, s, c)
    sine = jnp.where(odd, c, s)
    cosine = jnp.where(((quarter + 1) & 2) == 2, -cosine, cosine)
    sine = jnp.where((quarter & 2) == 2, -sine, sine)
    return cosine, sine


def encode(power):
    small = power < 2.0**-17
    scaled = jnp.where(small, power * -(2.0**80), power * 2.0**17)
    return (scaled * jnp.abs(scaled)).astype(jnp.bfloat16)


def decode(code):
    code = code.astype(jnp.float32)
    size = jnp.abs(code)
    root = size * lax.rsqrt(jnp.maximum(size, 2.0**-126))
    return root * jnp.where(code < 0, 2.0**-80, 2.0**-17)


def flip(me, m):
    bits = [lax.rem(me // b + m // b, 2) * b for b in (1, 2, 4, 8)]
    return bits[0] + bits[1] + bits[2] + bits[3]


def beam_kernel(
    n, volt_ref, gain_ref, cyl_ref, ns_ref, ew_ref, nb_ref, out_ref,
    volt, wide, gcol, ncol, dft, xin, x_ref,
    recv, wre, wim, sums, pbuf, precv,
    volt_sem, send_sem, recv_sem, own_sem, psend_sem, precv_sem, pown_sem,
):
    me = lax.axis_index("chan")

    def fetch(i):
        feeds = pl.ds(pl.multiple_of(i * 8, 8), 8)
        return pltpu.make_async_copy(volt_ref.at[:, feeds], volt.at[:, feeds], volt_sem.at[i])

    def begin(i, carry):
        fetch(i).start()
        return carry

    lax.fori_loop(0, 8, begin, 0)
    barrier = pltpu.get_barrier_semaphore()

    def greet(s, carry):
        pl.semaphore_signal(
            barrier, inc=1, device_id={"chan": lax.rem(me + s, n)}, device_id_type=MESH
        )
        return carry

    lax.fori_loop(1, n, greet, 0)

    row = lax.broadcasted_iota(jnp.int32, dft.shape, 0)
    col = lax.broadcasted_iota(jnp.int32, dft.shape, 1)
    same = (((row >> 6) & 1) == ((col >> 4) & 1)) & (((row >> 4) & 3) == ((col >> 5) & 3))
    turns = (row & 15) * (col & 15) * 32 + ((col >> 7) - (row >> 7)) * 128
    dft[...] = jnp.where(same, cos_sin(turns & 511)[0] * TWIDDLE, 0.0).astype(jnp.bfloat16)
    for r in range(2):
        for p in range(2):
            gcol[r, p] = jnp.broadcast_to(gain_ref[r, p : p + 1, :], (128, 64)).T

    def widen(i, carry):
        fetch(i).wait()
        first = pl.multiple_of(i * 8 * 2 * n, 8 * 2 * n)
        for r in range(2):
            for p in range(2):
                part = volt[r, pl.ds(pl.multiple_of(i * 8, 8), 8), p].astype(jnp.float32)
                part = part.reshape(8 * 2 * n, 256)
                for h in range(2):
                    wide[r, p, h, pl.ds(first, 8 * 2 * n), :] = part[:, h * 128 : (h + 1) * 128]
        return carry

    lax.fori_loop(0, 8, widen, 0)

    def volt_copy(g, m):
        d = flip(me, m)
        return pltpu.make_async_remote_copy(
            src_ref=x_ref.at[d, pl.ds(*GROUPS[g])],
            dst_ref=recv.at[pl.ds(*GROUPS[g]), me // 2, :, lax.rem(me, 2)],
            send_sem=send_sem.at[g, m],
            recv_sem=recv_sem.at[g, m],
            device_id={"chan": d},
            device_id_type=MESH,
        )

    def own_copy(g):
        return pltpu.make_async_copy(
            x_ref.at[me, pl.ds(*GROUPS[g])],
            recv.at[pl.ds(*GROUPS[g]), me // 2, :, lax.rem(me, 2)],
            own_sem.at[g],
        )

    def power_copy(g, m):
        d = flip(me, m)
        return pltpu.make_async_remote_copy(
            src_ref=pbuf.at[d, pl.ds(*GROUPS[g])],
            dst_ref=precv.at[me, pl.ds(*GROUPS[g])],
            send_sem=psend_sem.at[g, m],
            recv_sem=precv_sem.at[g, m],
            device_id={"chan": d},
            device_id_type=MESH,
        )

    def own_power(g):
        return pltpu.make_async_copy(
            pbuf.at[me, pl.ds(*GROUPS[g])], precv.at[me, pl.ds(*GROUPS[g])], pown_sem.at[g]
        )

    def partner(i):
        return lax.rem(i, 2) * lax.rem((i + 1) // 2, 8) + (1 - lax.rem(i, 2)) * (8 + i // 2)

    def each(make, act, g, partners=ORDER):
        for m in partners:
            getattr(make(g, m), act)()

    def produce(i, carry):
        m = partner(i)
        d = flip(me, m)
        for p in range(2):
            gr = gcol[0, p]
            gi = gcol[1, p]
            for c in range(2):
                for h in range(2):
                    at = pl.ds(d * 2 + c, 64, stride=2 * n)
                    real = wide[0, p, h, at, :]
                    imag = wide[1, p, h, at, :]
                    first = ((h * 2 + c) * 2 + p) * 64
                    xin[first : first + 64, :128] = (gr * real - gi * imag).astype(jnp.bfloat16)
                    xin[first : first + 64, 128:] = (gr * imag + gi * real).astype(jnp.bfloat16)
        bins = jnp.dot(xin[...], dft[...], preferred_element_type=jnp.float32)
        for q in range(PIECES):
            for p in range(2):
                part = bins[(q * 2 + p) * 64 : (q * 2 + p) * 64 + 64].astype(jnp.bfloat16)
                for r in range(2):
                    x_ref[d, q, r, :, p * 128 : (p + 1) * 128] = part[:, r * 128 : (r + 1) * 128]

        return carry

    def produce_and_send(i, carry):
        produce(i, carry)

        @pl.when(i < n - 1)
        def _():
            volt_copy(0, partner(i)).start()

        return carry

    lax.fori_loop(0, EARLY, produce, 0)
    pl.semaphore_wait(barrier, n - 1)
    each(volt_copy, "start", 0, ORDER[:EARLY])
    lax.fori_loop(EARLY, n, produce_and_send, 0)
    for g in range(2):
        own_copy(g).start()

    for h in range(2):
        ncol[h * 128 : (h + 1) * 128, :] = jnp.broadcast_to(nb_ref[h : h + 1, :], (128, 128)).T

    def table(i, carry):
        real = pl.ds(pl.multiple_of(i * 256, 256), 128)
        imag = pl.ds(pl.multiple_of(i * 256 + 128, 128), 128)
        cyl = cyl_ref[pl.ds(i, 1), :]
        ns = jnp.broadcast_to(ns_ref[pl.ds(i, 1), :], (128, 128))
        for h in range(2):
            slope = ns * ncol[h * 128 : (h + 1) * 128, :]
            for e in range(EWB):
                shift = jnp.where(
                    cyl < 2,
                    jnp.where(cyl == 0, ew_ref[e, 0], ew_ref[e, 1]),
                    jnp.where(cyl == 2, ew_ref[e, 2], ew_ref[e, 3]),
                )
                cosine, sine = cos_sin((slope + shift * 8) & 511)
                rows = slice(e * NSB + h * 128, e * NSB + h * 128 + 128)
                cosine = cosine.astype(jnp.bfloat16)
                wre[rows, real] = cosine
                wim[rows, imag] = cosine
                wim[rows, real] = sine.astype(jnp.bfloat16)
                wre[rows, imag] = (-sine).astype(jnp.bfloat16)
        return carry

    lax.fori_loop(0, FEEDS // 128, table, 0)
    blocks = BEAMS // 256
    lane = lax.broadcasted_iota(jnp.int32, (16, 128), 1)
    on = {w: (lane & w) != 0 for w in (16, 32, 64)}


    def finish(q, nb):
        for o in range(4):
            parts = []
            for g in range(4):
                at = pl.ds(pl.multiple_of(nb * 256 + o * 64 + g * 16, 16), 16)
                real = sums[q, 0, at, :]
                imag = sums[q, 1, at, :]
                power = real * real + imag * imag
                parts.append(power[:, :128] + power[:, 128:])
            halves = [
                jnp.where(on[64], b, a) + pltpu.roll(jnp.where(on[64], a, b), 64, 1)
                for a, b in ((parts[0], parts[2]), (parts[1], parts[3]))
            ]
            other = jnp.where(on[32], halves[0], halves[1])
            total = jnp.where(on[32], halves[1], halves[0]) + jnp.where(
                on[32], pltpu.roll(other, 32, 1), pltpu.roll(other, 96, 1)
            )
            pbuf[nb * 4 + o, q] = encode(total)

    def add(q, nb, first, tiles, fresh):
        rows = pl.ds(pl.multiple_of(nb * 256, 256), 256)
        terms = pl.ds(pl.multiple_of(first * 256, 256), tiles * 256)
        feeds = recv[q, pl.ds(first, tiles)].reshape(tiles * 256, 256)
        for r, weights in enumerate((wre, wim)):
            part = jnp.dot(weights[rows, terms], feeds, preferred_element_type=jnp.float32)
            sums[q, r, rows, :] = part if fresh else sums[q, r, rows, :] + part

    def beams(body):
        def one(i, carry):
            body(lax.rem(i + (1 - me // 8) * 2, blocks))
            return carry

        lax.fori_loop(0, blocks, one, 0)

    each(volt_copy, "start", 1, (8, 12, 1, 9, 13, 2, 10, 14, 3, 11, 15, 4, 5, 6, 7))
    near = me // 8 * 4
    far = (flip(me, 8) // 4 * 2, flip(me, 12) // 4 * 2)
    for g in range(2):
        own_copy(g).wait()
        each(volt_copy, "wait_recv", g, range(1, 8))
        for q in range(GROUPS[g][0], sum(GROUPS[g])):
            beams(lambda nb, q=q: add(q, nb, near, 4, True))
    each(volt_copy, "wait_recv", 0, range(8, 12))
    for q in range(3):
        beams(lambda nb, q=q: add(q, nb, far[0], 2, False))
    each(volt_copy, "wait_recv", 0, range(12, 16))
    for q in range(3):

        def whole(nb, q=q):
            add(q, nb, far[1], 2, False)
            finish(q, nb)

        beams(whole)
    each(power_copy, "start", 0)
    own_power(0).start()
    each(volt_copy, "wait_recv", 1, range(8, 12))
    beams(lambda nb: add(3, nb, far[0], 2, False))
    each(volt_copy, "wait_recv", 1, range(12, 16))

    def last(nb):
        add(3, nb, far[1], 2, False)
        finish(3, nb)
        for o in range(4):
            m = flip(me, nb * 4 + o)

            @pl.when(m > 0)
            def _(m=m):
                power_copy(1, m).start()

    beams(last)
    own_power(1).start()
    each(volt_copy, "wait_send", 0)
    each(volt_copy, "wait_send", 1)

    for h in range(2):
        each(power_copy, "wait_recv", h)
        own_power(h).wait()
        tiles = []
        for t in range(4):
            vals = [
                decode(precv[4 * t + s, h * 2 + c]) for s in range(4) for c in range(2)
            ]
            for b in range(3):
                w = 16 << b
                for a in range(8):
                    if not a >> b & 1:
                        z = a | 1 << b
                        vals[a], vals[z] = (
                            jnp.where(on[w], pltpu.roll(vals[z], w, 1), vals[a]),
                            jnp.where(on[w], vals[z], pltpu.roll(vals[a], 128 - w, 1)),
                        )
            tiles.append(vals)
        for a in range(8):
            total = tiles[0][a] + tiles[1][a] + tiles[2][a] + tiles[3][a]
            baseline = jnp.sum(total, axis=1, keepdims=True) * (1.0 / (n * 32))
            scale = 1.0 / (baseline + eps_power * TWIDDLE_GAIN**2)
            for t in range(4):
                at = (a >> 1) * 256 + t * 4 + h * 2 + (a & 1)
                out_ref[pl.ds(at, 16, stride=16), :] = tiles[t][a] * scale
    for g in range(2):
        each(power_copy, "wait_send", g)


def fused(n, voltages, gains, feed_cyl, feed_ns, ew_index, ns_beam):
    vmem = pl.BlockSpec(memory_space=pltpu.VMEM)
    dma = pltpu.SemaphoreType.DMA
    out = pl.pallas_call(
        functools.partial(beam_kernel, n),
        out_shape=pltpu.VMEM((1024, 128), jnp.float32),
        in_specs=[
            pl.BlockSpec(memory_space=pl.ANY), vmem, vmem, vmem,
            pl.BlockSpec(memory_space=pltpu.SMEM), vmem,
        ],
        out_specs=vmem,
        scratch_shapes=[
            pltpu.VMEM(voltages.shape, jnp.bfloat16),
            pltpu.VMEM((2, 2, 2, 64 * 2 * n, 128), jnp.float32),
            pltpu.VMEM((2, 2, 64, 128), jnp.float32),
            pltpu.VMEM((NSB, 128), jnp.int32),
            pltpu.VMEM((256, 256), jnp.bfloat16),
            pltpu.VMEM((512, 256), jnp.bfloat16),
            pltpu.VMEM((n, PIECES, 2, 64, 256), jnp.bfloat16),
            pltpu.VMEM((PIECES, n // 2, 2, 2, 64, 256), jnp.bfloat16),
            pltpu.VMEM((BEAMS, 2 * FEEDS), jnp.bfloat16),
            pltpu.VMEM((BEAMS, 2 * FEEDS), jnp.bfloat16),
            pltpu.VMEM((PIECES, 2, BEAMS, 256), jnp.float32),
            pltpu.VMEM((n, PIECES, 16, 128), jnp.bfloat16),
            pltpu.VMEM((n, PIECES, 16, 128), jnp.bfloat16),
            dma((8,)), dma((2, n)), dma((2, n)), dma((2,)),
            dma((2, n)), dma((2, n)), dma((2,)),
        ],
        compiler_params=pltpu.CompilerParams(
            collective_id=0, has_side_effects=True, vmem_limit_bytes=56 << 20
        ),
    )(
        voltages, gains, feed_cyl.reshape(-1, 128), feed_ns.reshape(-1, 128),
        ew_index, ns_beam.reshape(-1, 128),
    )
    return out.reshape(64, 4, TOUT, 128).transpose(0, 2, 1, 3).reshape(64, TOUT, 512)


def solution(mesh):
    placed = (P(None, "chan", None, None, "grp"), P(None, None, "chan"), P(), P(), P(), P())
    n = mesh.shape["chan"]

    def part(voltages, gains, feed_cyl, feed_ns, ew_index, ns_beam):
        fits = voltages.shape == (2, 64, 2, 2 * n, UP * DS * TOUT) and n * 64 == FEEDS
        run = functools.partial(fused, n) if fits else shards
        return run(voltages, gains, feed_cyl, feed_ns, ew_index, ns_beam)

    return jax.shard_map(
        part, mesh=mesh, in_specs=placed, out_specs=P("chan", "grp", None), check_vma=False
    )
```

```python
import functools
import math

import jax
import jax.numpy as jnp
from jax import lax
from jax.experimental import pallas as pl
from jax.experimental.pallas import tpu as pltpu
from jax.sharding import PartitionSpec as P

CYL = 4
NSF = 256
EWB = 4
NSB = 256
EW_PH = 64
UP = 16
DS = 4
FEEDS = 1024
BEAMS = 1024
TOUT = 4


eps_power = 1e-06
MESH = pl.DeviceIdType.MESH
PIECES = 4
EARLY = 1
GROUPS = ((0, 3), (3, 1))
ORDER = (8, 9, 10, 11, 12, 13, 14, 15, 1, 2, 3, 4, 5, 6, 7)
TWIDDLE = 1.1305
TWIDDLE_GAIN = 1.132804


def phase_table(feed_cyl, feed_ns, ew_index, ns_beam):
    modulus = 2 * NSF * EW_PH
    cyl_onehot = (feed_cyl[:, None] == jnp.arange(CYL, dtype=jnp.int32)[None, :]).astype(jnp.int32)
    ew_term = jnp.sum(cyl_onehot[:, None, :] * ew_index[None, :, :], axis=2)
    ns_term = feed_ns[:, None] * ns_beam[None, :] * EW_PH
    steps_int = (ew_term[:, :, None] * (2 * NSF) + ns_term[:, None, :]) % modulus
    angles = steps_int.reshape(FEEDS, EWB * NSB).astype(jnp.float32) * (2.0 * math.pi / modulus)
    cosine = jnp.cos(angles).astype(jnp.bfloat16)
    sine_part = jnp.sin(angles).astype(jnp.bfloat16)
    upper_rows = jnp.concatenate([cosine, sine_part], axis=1)
    lower_rows = jnp.concatenate([-sine_part, cosine], axis=1)
    return jnp.concatenate([upper_rows, lower_rows], axis=0)


def upchannel_table():
    bin_index = jnp.arange(UP, dtype=jnp.int32)
    angles = (bin_index[:, None] * bin_index[None, :] % UP).astype(jnp.float32) * (
        2.0 * math.pi / UP
    )
    cosine = jnp.cos(angles)
    sine_part = jnp.sin(angles)
    return jnp.stack([jnp.stack([cosine, -sine_part], -1), jnp.stack([sine_part, cosine], -1)], 1)


def shards(voltages, gains, feed_cyl, feed_ns, ew_index, ns_beam):
    weights = phase_table(feed_cyl, feed_ns, ew_index, ns_beam).reshape(2, FEEDS, 2 * BEAMS)
    fine_table = upchannel_table()
    sample = voltages.astype(jnp.float32)
    gain_real = gains[0].T[:, :, None, None]
    gain_imag = gains[1].T[:, :, None, None]
    calibrated = jnp.stack(
        [
            (gain_real * sample[0] - gain_imag * sample[1]).astype(jnp.bfloat16),
            (gain_real * sample[1] + gain_imag * sample[0]).astype(jnp.bfloat16),
        ]
    )
    arrived = lax.all_to_all(calibrated, "chan", split_axis=3, concat_axis=1, tiled=True)
    pieces = arrived.shape[2]
    channels = arrived.shape[3]
    beam_sums = jnp.einsum("rfpct,rfq->pctq", arrived, weights, preferred_element_type=jnp.float32)
    beam_sums = beam_sums.reshape(pieces, channels, TOUT, DS, UP, 2, BEAMS)
    fine_bins = jnp.einsum(
        "pcudjrb,jrks->pbudcks", beam_sums, fine_table, precision=lax.Precision.HIGHEST
    )
    beam_power = jnp.sum(jnp.sum(fine_bins * fine_bins, axis=(3, 6)), axis=0)
    total_chans = beam_power.shape[2] * lax.axis_size("chan")
    band_sum = lax.psum(jnp.sum(beam_power, axis=(2, 3)), "chan")
    baseline = band_sum / (total_chans * UP)
    normed = beam_power / (baseline[:, :, None, None] + eps_power)
    intensity = lax.all_to_all(normed, "chan", split_axis=0, concat_axis=2, tiled=True)
    return intensity.reshape(intensity.shape[0], TOUT, intensity.shape[2] * UP)


def cos_sin(steps):
    quarter = (steps + 64) >> 7
    x = (steps - (quarter << 7)).astype(jnp.float32) * (2.0 * math.pi / 512)
    y = x * x
    s = x * (1.0 + y * (-1 / 6 + y * (1 / 120 + y * (-1 / 5040 + y * (1 / 362880)))))
    c = 1.0 + y * (-0.5 + y * (1 / 24 + y * (-1 / 720 + y * (1 / 40320))))
    odd = (quarter & 1) == 1
    cosine = jnp.where(odd, s, c)
    sine = jnp.where(odd, c, s)
    cosine = jnp.where(((quarter + 1) & 2) == 2, -cosine, cosine)
    sine = jnp.where((quarter & 2) == 2, -sine, sine)
    return cosine, sine


def encode(power):
    small = power < 2.0**-17
    scaled = jnp.where(small, power * -(2.0**80), power * 2.0**17)
    return (scaled * jnp.abs(scaled)).astype(jnp.bfloat16)


def decode(code):
    code = code.astype(jnp.float32)
    size = jnp.abs(code)
    root = size * lax.rsqrt(jnp.maximum(size, 2.0**-126))
    return root * jnp.where(code < 0, 2.0**-80, 2.0**-17)


def flip(me, m):
    bits = [lax.rem(me // b + m // b, 2) * b for b in (1, 2, 4, 8)]
    return bits[0] + bits[1] + bits[2] + bits[3]


def beam_kernel(
    n, volt_ref, gain_ref, cyl_ref, ns_ref, ew_ref, nb_ref, out_ref,
    volt, wide, gcol, ncol, dft, xin, x_ref,
    recv, wre, wim, sums, pbuf, precv,
    volt_sem, send_sem, recv_sem, own_sem, psend_sem, precv_sem, pown_sem,
):
    me = lax.axis_index("chan")

    def fetch(i):
        feeds = pl.ds(pl.multiple_of(i * 8, 8), 8)
        return pltpu.make_async_copy(volt_ref.at[:, feeds], volt.at[:, feeds], volt_sem.at[i])

    def begin(i, carry):
        fetch(i).start()
        return carry

    lax.fori_loop(0, 8, begin, 0)
    barrier = pltpu.get_barrier_semaphore()

    def greet(s, carry):
        pl.semaphore_signal(
            barrier, inc=1, device_id={"chan": lax.rem(me + s, n)}, device_id_type=MESH
        )
        return carry

    lax.fori_loop(1, n, greet, 0)

    row = lax.broadcasted_iota(jnp.int32, dft.shape, 0)
    col = lax.broadcasted_iota(jnp.int32, dft.shape, 1)
    same = (((row >> 6) & 1) == ((col >> 4) & 1)) & (((row >> 4) & 3) == ((col >> 5) & 3))
    turns = (row & 15) * (col & 15) * 32 + ((col >> 7) - (row >> 7)) * 128
    dft[...] = jnp.where(same, cos_sin(turns & 511)[0] * TWIDDLE, 0.0).astype(jnp.bfloat16)
    for r in range(2):
        for p in range(2):
            gcol[r, p] = jnp.broadcast_to(gain_ref[r, p : p + 1, :], (128, 64)).T

    def widen(i, carry):
        fetch(i).wait()
        first = pl.multiple_of(i * 8 * 2 * n, 8 * 2 * n)
        for r in range(2):
            for p in range(2):
                part = volt[r, pl.ds(pl.multiple_of(i * 8, 8), 8), p].astype(jnp.float32)
                part = part.reshape(8 * 2 * n, 256)
                for h in range(2):
                    wide[r, p, h, pl.ds(first, 8 * 2 * n), :] = part[:, h * 128 : (h + 1) * 128]
        return carry

    lax.fori_loop(0, 8, widen, 0)

    def volt_copy(g, m):
        d = flip(me, m)
        return pltpu.make_async_remote_copy(
            src_ref=x_ref.at[d, pl.ds(*GROUPS[g])],
            dst_ref=recv.at[pl.ds(*GROUPS[g]), me // 2, :, lax.rem(me, 2)],
            send_sem=send_sem.at[g, m],
            recv_sem=recv_sem.at[g, m],
            device_id={"chan": d},
            device_id_type=MESH,
        )

    def own_copy(g):
        return pltpu.make_async_copy(
            x_ref.at[me, pl.ds(*GROUPS[g])],
            recv.at[pl.ds(*GROUPS[g]), me // 2, :, lax.rem(me, 2)],
            own_sem.at[g],
        )

    def power_copy(g, m):
        d = flip(me, m)
        return pltpu.make_async_remote_copy(
            src_ref=pbuf.at[d, pl.ds(*GROUPS[g])],
            dst_ref=precv.at[me, pl.ds(*GROUPS[g])],
            send_sem=psend_sem.at[g, m],
            recv_sem=precv_sem.at[g, m],
            device_id={"chan": d},
            device_id_type=MESH,
        )

    def own_power(g):
        return pltpu.make_async_copy(
            pbuf.at[me, pl.ds(*GROUPS[g])], precv.at[me, pl.ds(*GROUPS[g])], pown_sem.at[g]
        )

    def partner(i):
        return (1 - i // 8) * (8 + i) + i // 8 * lax.rem(i + 1, 8)

    def each(make, act, g, partners=ORDER):
        for m in partners:
            getattr(make(g, m), act)()

    def produce(i, carry):
        m = partner(i)
        d = flip(me, m)
        for p in range(2):
            gr = gcol[0, p]
            gi = gcol[1, p]
            for c in range(2):
                for h in range(2):
                    at = pl.ds(d * 2 + c, 64, stride=2 * n)
                    real = wide[0, p, h, at, :]
                    imag = wide[1, p, h, at, :]
                    first = ((h * 2 + c) * 2 + p) * 64
                    xin[first : first + 64, :128] = (gr * real - gi * imag).astype(jnp.bfloat16)
                    xin[first : first + 64, 128:] = (gr * imag + gi * real).astype(jnp.bfloat16)
        bins = jnp.dot(xin[...], dft[...], preferred_element_type=jnp.float32)
        for q in range(PIECES):
            for p in range(2):
                part = bins[(q * 2 + p) * 64 : (q * 2 + p) * 64 + 64].astype(jnp.bfloat16)
                for r in range(2):
                    x_ref[d, q, r, :, p * 128 : (p + 1) * 128] = part[:, r * 128 : (r + 1) * 128]

        return carry

    def produce_and_send(i, carry):
        produce(i, carry)

        @pl.when(i < n - 1)
        def _():
            volt_copy(0, partner(i)).start()

        return carry

    lax.fori_loop(0, EARLY, produce, 0)
    pl.semaphore_wait(barrier, n - 1)
    each(volt_copy, "start", 0, ORDER[:EARLY])
    lax.fori_loop(EARLY, n, produce_and_send, 0)
    for g in range(2):
        own_copy(g).start()

    for h in range(2):
        ncol[h * 128 : (h + 1) * 128, :] = jnp.broadcast_to(nb_ref[h : h + 1, :], (128, 128)).T

    def table(i, carry):
        real = pl.ds(pl.multiple_of(i * 256, 256), 128)
        imag = pl.ds(pl.multiple_of(i * 256 + 128, 128), 128)
        cyl = cyl_ref[pl.ds(i, 1), :]
        ns = jnp.broadcast_to(ns_ref[pl.ds(i, 1), :], (128, 128))
        for h in range(2):
            slope = ns * ncol[h * 128 : (h + 1) * 128, :]
            for e in range(EWB):
                shift = jnp.where(
                    cyl < 2,
                    jnp.where(cyl == 0, ew_ref[e, 0], ew_ref[e, 1]),
                    jnp.where(cyl == 2, ew_ref[e, 2], ew_ref[e, 3]),
                )
                cosine, sine = cos_sin((slope + shift * 8) & 511)
                rows = slice(e * NSB + h * 128, e * NSB + h * 128 + 128)
                cosine = cosine.astype(jnp.bfloat16)
                wre[rows, real] = cosine
                wim[rows, imag] = cosine
                wim[rows, real] = sine.astype(jnp.bfloat16)
                wre[rows, imag] = (-sine).astype(jnp.bfloat16)
        return carry

    lax.fori_loop(0, FEEDS // 128, table, 0)
    blocks = BEAMS // 256
    lane = lax.broadcasted_iota(jnp.int32, (16, 128), 1)
    on = {w: (lane & w) != 0 for w in (16, 32, 64)}


    def finish(q, nb):
        for o in range(4):
            parts = []
            for g in range(4):
                at = pl.ds(pl.multiple_of(nb * 256 + o * 64 + g * 16, 16), 16)
                real = sums[q, 0, at, :]
                imag = sums[q, 1, at, :]
                power = real * real + imag * imag
                parts.append(power[:, :128] + power[:, 128:])
            halves = [
                jnp.where(on[64], b, a) + pltpu.roll(jnp.where(on[64], a, b), 64, 1)
                for a, b in ((parts[0], parts[2]), (parts[1], parts[3]))
            ]
            other = jnp.where(on[32], halves[0], halves[1])
            total = jnp.where(on[32], halves[1], halves[0]) + jnp.where(
                on[32], pltpu.roll(other, 32, 1), pltpu.roll(other, 96, 1)
            )
            pbuf[nb * 4 + o, q] = encode(total)

    def add(q, nb, first, tiles, fresh):
        rows = pl.ds(pl.multiple_of(nb * 256, 256), 256)
        terms = pl.ds(pl.multiple_of(first * 256, 256), tiles * 256)
        feeds = recv[q, pl.ds(first, tiles)].reshape(tiles * 256, 256)
        for r, weights in enumerate((wre, wim)):
            part = jnp.dot(weights[rows, terms], feeds, preferred_element_type=jnp.float32)
            sums[q, r, rows, :] = part if fresh else sums[q, r, rows, :] + part

    def beams(body):
        def one(i, carry):
            body(lax.rem(i + (1 - me // 8) * 2, blocks))
            return carry

        lax.fori_loop(0, blocks, one, 0)

    each(volt_copy, "start", 1, (8, 12, 1, 9, 13, 2, 10, 14, 3, 11, 15, 4, 5, 6, 7))
    near = me // 8 * 4
    far = (flip(me, 8) // 4 * 2, flip(me, 12) // 4 * 2)
    for g in range(2):
        own_copy(g).wait()
        each(volt_copy, "wait_recv", g, range(1, 8))
        for q in range(GROUPS[g][0], sum(GROUPS[g])):
            beams(lambda nb, q=q: add(q, nb, near, 4, True))
    each(volt_copy, "wait_recv", 0, range(8, 12))
    for q in range(3):
        beams(lambda nb, q=q: add(q, nb, far[0], 2, False))
    each(volt_copy, "wait_recv", 0, range(12, 16))
    for q in range(3):

        def whole(nb, q=q):
            add(q, nb, far[1], 2, False)
            finish(q, nb)

        beams(whole)
    each(power_copy, "start", 0)
    own_power(0).start()
    each(volt_copy, "wait_recv", 1, range(8, 12))
    beams(lambda nb: add(3, nb, far[0], 2, False))
    each(volt_copy, "wait_recv", 1, range(12, 16))

    def last(nb):
        add(3, nb, far[1], 2, False)
        finish(3, nb)
        for o in range(4):
            m = flip(me, nb * 4 + o)

            @pl.when(m > 0)
            def _(m=m):
                power_copy(1, m).start()

    beams(last)
    own_power(1).start()
    each(volt_copy, "wait_send", 0)
    each(volt_copy, "wait_send", 1)

    for h in range(2):
        each(power_copy, "wait_recv", h)
        own_power(h).wait()
        tiles = []
        for t in range(4):
            vals = [
                decode(precv[4 * t + s, h * 2 + c]) for s in range(4) for c in range(2)
            ]
            for b in range(3):
                w = 16 << b
                for a in range(8):
                    if not a >> b & 1:
                        z = a | 1 << b
                        vals[a], vals[z] = (
                            jnp.where(on[w], pltpu.roll(vals[z], w, 1), vals[a]),
                            jnp.where(on[w], vals[z], pltpu.roll(vals[a], 128 - w, 1)),
                        )
            tiles.append(vals)
        for a in range(8):
            total = tiles[0][a] + tiles[1][a] + tiles[2][a] + tiles[3][a]
            baseline = jnp.sum(total, axis=1, keepdims=True) * (1.0 / (n * 32))
            scale = 1.0 / (baseline + eps_power * TWIDDLE_GAIN**2)
            for t in range(4):
                at = (a >> 1) * 256 + t * 4 + h * 2 + (a & 1)
                out_ref[pl.ds(at, 16, stride=16), :] = tiles[t][a] * scale
    for g in range(2):
        each(power_copy, "wait_send", g)


def fused(n, voltages, gains, feed_cyl, feed_ns, ew_index, ns_beam):
    vmem = pl.BlockSpec(memory_space=pltpu.VMEM)
    dma = pltpu.SemaphoreType.DMA
    out = pl.pallas_call(
        functools.partial(beam_kernel, n),
        out_shape=pltpu.VMEM((1024, 128), jnp.float32),
        in_specs=[
            pl.BlockSpec(memory_space=pl.ANY), vmem, vmem, vmem,
            pl.BlockSpec(memory_space=pltpu.SMEM), vmem,
        ],
        out_specs=vmem,
        scratch_shapes=[
            pltpu.VMEM(voltages.shape, jnp.bfloat16),
            pltpu.VMEM((2, 2, 2, 64 * 2 * n, 128), jnp.float32),
            pltpu.VMEM((2, 2, 64, 128), jnp.float32),
            pltpu.VMEM((NSB, 128), jnp.int32),
            pltpu.VMEM((256, 256), jnp.bfloat16),
            pltpu.VMEM((512, 256), jnp.bfloat16),
            pltpu.VMEM((n, PIECES, 2, 64, 256), jnp.bfloat16),
            pltpu.VMEM((PIECES, n // 2, 2, 2, 64, 256), jnp.bfloat16),
            pltpu.VMEM((BEAMS, 2 * FEEDS), jnp.bfloat16),
            pltpu.VMEM((BEAMS, 2 * FEEDS), jnp.bfloat16),
            pltpu.VMEM((PIECES, 2, BEAMS, 256), jnp.float32),
            pltpu.VMEM((n, PIECES, 16, 128), jnp.bfloat16),
            pltpu.VMEM((n, PIECES, 16, 128), jnp.bfloat16),
            dma((8,)), dma((2, n)), dma((2, n)), dma((2,)),
            dma((2, n)), dma((2, n)), dma((2,)),
        ],
        compiler_params=pltpu.CompilerParams(
            collective_id=0, has_side_effects=True, vmem_limit_bytes=56 << 20
        ),
    )(
        voltages, gains, feed_cyl.reshape(-1, 128), feed_ns.reshape(-1, 128),
        ew_index, ns_beam.reshape(-1, 128),
    )
    return out.reshape(64, 4, TOUT, 128).transpose(0, 2, 1, 3).reshape(64, TOUT, 512)


def solution(mesh):
    placed = (P(None, "chan", None, None, "grp"), P(None, None, "chan"), P(), P(), P(), P())
    n = mesh.shape["chan"]

    def part(voltages, gains, feed_cyl, feed_ns, ew_index, ns_beam):
        fits = voltages.shape == (2, 64, 2, 2 * n, UP * DS * TOUT) and n * 64 == FEEDS
        run = functools.partial(fused, n) if fits else shards
        return run(voltages, gains, feed_cyl, feed_ns, ew_index, ns_beam)

    return jax.shard_map(
        part, mesh=mesh, in_specs=placed, out_specs=P("chan", "grp", None), check_vma=False
    )
```

```python
import functools
import math

import jax
import jax.numpy as jnp
from jax import lax
from jax.experimental import pallas as pl
from jax.experimental.pallas import tpu as pltpu
from jax.sharding import PartitionSpec as P

CYL = 4
NSF = 256
EWB = 4
NSB = 256
EW_PH = 64
UP = 16
DS = 4
FEEDS = 1024
BEAMS = 1024
TOUT = 4


eps_power = 1e-06
MESH = pl.DeviceIdType.MESH
PIECES = 4
EARLY = 1
GROUPS = ((0, 3), (3, 1))
ORDER = (8, 1, 9, 2, 10, 3, 11, 4, 12, 5, 13, 6, 14, 7, 15)
TWIDDLE = 1.1305
TWIDDLE_GAIN = 1.132804


def phase_table(feed_cyl, feed_ns, ew_index, ns_beam):
    modulus = 2 * NSF * EW_PH
    cyl_onehot = (feed_cyl[:, None] == jnp.arange(CYL, dtype=jnp.int32)[None, :]).astype(jnp.int32)
    ew_term = jnp.sum(cyl_onehot[:, None, :] * ew_index[None, :, :], axis=2)
    ns_term = feed_ns[:, None] * ns_beam[None, :] * EW_PH
    steps_int = (ew_term[:, :, None] * (2 * NSF) + ns_term[:, None, :]) % modulus
    angles = steps_int.reshape(FEEDS, EWB * NSB).astype(jnp.float32) * (2.0 * math.pi / modulus)
    cosine = jnp.cos(angles).astype(jnp.bfloat16)
    sine_part = jnp.sin(angles).astype(jnp.bfloat16)
    upper_rows = jnp.concatenate([cosine, sine_part], axis=1)
    lower_rows = jnp.concatenate([-sine_part, cosine], axis=1)
    return jnp.concatenate([upper_rows, lower_rows], axis=0)


def upchannel_table():
    bin_index = jnp.arange(UP, dtype=jnp.int32)
    angles = (bin_index[:, None] * bin_index[None, :] % UP).astype(jnp.float32) * (
        2.0 * math.pi / UP
    )
    cosine = jnp.cos(angles)
    sine_part = jnp.sin(angles)
    return jnp.stack([jnp.stack([cosine, -sine_part], -1), jnp.stack([sine_part, cosine], -1)], 1)


def shards(voltages, gains, feed_cyl, feed_ns, ew_index, ns_beam):
    weights = phase_table(feed_cyl, feed_ns, ew_index, ns_beam).reshape(2, FEEDS, 2 * BEAMS)
    fine_table = upchannel_table()
    sample = voltages.astype(jnp.float32)
    gain_real = gains[0].T[:, :, None, None]
    gain_imag = gains[1].T[:, :, None, None]
    calibrated = jnp.stack(
        [
            (gain_real * sample[0] - gain_imag * sample[1]).astype(jnp.bfloat16),
            (gain_real * sample[1] + gain_imag * sample[0]).astype(jnp.bfloat16),
        ]
    )
    arrived = lax.all_to_all(calibrated, "chan", split_axis=3, concat_axis=1, tiled=True)
    pieces = arrived.shape[2]
    channels = arrived.shape[3]
    beam_sums = jnp.einsum("rfpct,rfq->pctq", arrived, weights, preferred_element_type=jnp.float32)
    beam_sums = beam_sums.reshape(pieces, channels, TOUT, DS, UP, 2, BEAMS)
    fine_bins = jnp.einsum(
        "pcudjrb,jrks->pbudcks", beam_sums, fine_table, precision=lax.Precision.HIGHEST
    )
    beam_power = jnp.sum(jnp.sum(fine_bins * fine_bins, axis=(3, 6)), axis=0)
    total_chans = beam_power.shape[2] * lax.axis_size("chan")
    band_sum = lax.psum(jnp.sum(beam_power, axis=(2, 3)), "chan")
    baseline = band_sum / (total_chans * UP)
    normed = beam_power / (baseline[:, :, None, None] + eps_power)
    intensity = lax.all_to_all(normed, "chan", split_axis=0, concat_axis=2, tiled=True)
    return intensity.reshape(intensity.shape[0], TOUT, intensity.shape[2] * UP)


def cos_sin(steps):
    quarter = (steps + 64) >> 7
    x = (steps - (quarter << 7)).astype(jnp.float32) * (2.0 * math.pi / 512)
    y = x * x
    s = x * (1.0 + y * (-1 / 6 + y * (1 / 120 + y * (-1 / 5040 + y * (1 / 362880)))))
    c = 1.0 + y * (-0.5 + y * (1 / 24 + y * (-1 / 720 + y * (1 / 40320))))
    odd = (quarter & 1) == 1
    cosine = jnp.where(odd, s, c)
    sine = jnp.where(odd, c, s)
    cosine = jnp.where(((quarter + 1) & 2) == 2, -cosine, cosine)
    sine = jnp.where((quarter & 2) == 2, -sine, sine)
    return cosine, sine


def encode(power):
    small = power < 2.0**-17
    scaled = jnp.where(small, power * -(2.0**80), power * 2.0**17)
    return (scaled * jnp.abs(scaled)).astype(jnp.bfloat16)


def decode(code):
    code = code.astype(jnp.float32)
    size = jnp.abs(code)
    root = size * lax.rsqrt(jnp.maximum(size, 2.0**-126))
    return root * jnp.where(code < 0, 2.0**-80, 2.0**-17)


def flip(me, m):
    bits = [lax.rem(me // b + m // b, 2) * b for b in (1, 2, 4, 8)]
    return bits[0] + bits[1] + bits[2] + bits[3]


def beam_kernel(
    n, volt_ref, gain_ref, cyl_ref, ns_ref, ew_ref, nb_ref, out_ref,
    volt, wide, gcol, ncol, dft, xin, x_ref,
    recv, wre, wim, sums, pbuf, precv,
    volt_sem, send_sem, recv_sem, own_sem, psend_sem, precv_sem, pown_sem,
):
    me = lax.axis_index("chan")

    def fetch(i):
        feeds = pl.ds(pl.multiple_of(i * 8, 8), 8)
        return pltpu.make_async_copy(volt_ref.at[:, feeds], volt.at[:, feeds], volt_sem.at[i])

    def begin(i, carry):
        fetch(i).start()
        return carry

    lax.fori_loop(0, 8, begin, 0)
    barrier = pltpu.get_barrier_semaphore()

    def greet(s, carry):
        pl.semaphore_signal(
            barrier, inc=1, device_id={"chan": lax.rem(me + s, n)}, device_id_type=MESH
        )
        return carry

    lax.fori_loop(1, n, greet, 0)

    row = lax.broadcasted_iota(jnp.int32, dft.shape, 0)
    col = lax.broadcasted_iota(jnp.int32, dft.shape, 1)
    same = (((row >> 6) & 1) == ((col >> 4) & 1)) & (((row >> 4) & 3) == ((col >> 5) & 3))
    turns = (row & 15) * (col & 15) * 32 + ((col >> 7) - (row >> 7)) * 128
    dft[...] = jnp.where(same, cos_sin(turns & 511)[0] * TWIDDLE, 0.0).astype(jnp.bfloat16)
    for r in range(2):
        for p in range(2):
            gcol[r, p] = jnp.broadcast_to(gain_ref[r, p : p + 1, :], (128, 64)).T

    def widen(i, carry):
        fetch(i).wait()
        first = pl.multiple_of(i * 8 * 2 * n, 8 * 2 * n)
        for r in range(2):
            for p in range(2):
                part = volt[r, pl.ds(pl.multiple_of(i * 8, 8), 8), p].astype(jnp.float32)
                part = part.reshape(8 * 2 * n, 256)
                for h in range(2):
                    wide[r, p, h, pl.ds(first, 8 * 2 * n), :] = part[:, h * 128 : (h + 1) * 128]
        return carry

    lax.fori_loop(0, 8, widen, 0)

    def volt_copy(g, m):
        d = flip(me, m)
        return pltpu.make_async_remote_copy(
            src_ref=x_ref.at[d, pl.ds(*GROUPS[g])],
            dst_ref=recv.at[pl.ds(*GROUPS[g]), me // 2, :, lax.rem(me, 2)],
            send_sem=send_sem.at[g, m],
            recv_sem=recv_sem.at[g, m],
            device_id={"chan": d},
            device_id_type=MESH,
        )

    def own_copy(g):
        return pltpu.make_async_copy(
            x_ref.at[me, pl.ds(*GROUPS[g])],
            recv.at[pl.ds(*GROUPS[g]), me // 2, :, lax.rem(me, 2)],
            own_sem.at[g],
        )

    def power_copy(g, m):
        d = flip(me, m)
        return pltpu.make_async_remote_copy(
            src_ref=pbuf.at[d, pl.ds(*GROUPS[g])],
            dst_ref=precv.at[me, pl.ds(*GROUPS[g])],
            send_sem=psend_sem.at[g, m],
            recv_sem=precv_sem.at[g, m],
            device_id={"chan": d},
            device_id_type=MESH,
        )

    def own_power(g):
        return pltpu.make_async_copy(
            pbuf.at[me, pl.ds(*GROUPS[g])], precv.at[me, pl.ds(*GROUPS[g])], pown_sem.at[g]
        )

    def partner(i):
        return lax.rem(i, 2) * lax.rem((i + 1) // 2, 8) + (1 - lax.rem(i, 2)) * (8 + i // 2)

    def each(make, act, g, partners=ORDER):
        for m in partners:
            getattr(make(g, m), act)()

    def produce(i, carry):
        m = partner(i)
        d = flip(me, m)
        for p in range(2):
            gr = gcol[0, p]
            gi = gcol[1, p]
            for c in range(2):
                for h in range(2):
                    at = pl.ds(d * 2 + c, 64, stride=2 * n)
                    real = wide[0, p, h, at, :]
                    imag = wide[1, p, h, at, :]
                    first = ((h * 2 + c) * 2 + p) * 64
                    xin[first : first + 64, :128] = (gr * real - gi * imag).astype(jnp.bfloat16)
                    xin[first : first + 64, 128:] = (gr * imag + gi * real).astype(jnp.bfloat16)
        bins = jnp.dot(xin[...], dft[...], preferred_element_type=jnp.float32)
        for q in range(PIECES):
            for p in range(2):
                part = bins[(q * 2 + p) * 64 : (q * 2 + p) * 64 + 64].astype(jnp.bfloat16)
                for r in range(2):
                    x_ref[d, q, r, :, p * 128 : (p + 1) * 128] = part[:, r * 128 : (r + 1) * 128]

        return carry

    def produce_and_send(i, carry):
        produce(i, carry)

        @pl.when(i < n - 1)
        def _():
            volt_copy(0, partner(i)).start()

        return carry

    lax.fori_loop(0, EARLY, produce, 0)
    pl.semaphore_wait(barrier, n - 1)
    each(volt_copy, "start", 0, ORDER[:EARLY])
    lax.fori_loop(EARLY, n, produce_and_send, 0)
    for g in range(2):
        own_copy(g).start()

    for h in range(2):
        ncol[h * 128 : (h + 1) * 128, :] = jnp.broadcast_to(nb_ref[h : h + 1, :], (128, 128)).T

    def table(i, carry):
        real = pl.ds(pl.multiple_of(i * 256, 256), 128)
        imag = pl.ds(pl.multiple_of(i * 256 + 128, 128), 128)
        cyl = cyl_ref[pl.ds(i, 1), :]
        ns = jnp.broadcast_to(ns_ref[pl.ds(i, 1), :], (128, 128))
        for h in range(2):
            slope = ns * ncol[h * 128 : (h + 1) * 128, :]
            for e in range(EWB):
                shift = jnp.where(
                    cyl < 2,
                    jnp.where(cyl == 0, ew_ref[e, 0], ew_ref[e, 1]),
                    jnp.where(cyl == 2, ew_ref[e, 2], ew_ref[e, 3]),
                )
                cosine, sine = cos_sin((slope + shift * 8) & 511)
                rows = slice(e * NSB + h * 128, e * NSB + h * 128 + 128)
                cosine = cosine.astype(jnp.bfloat16)
                wre[rows, real] = cosine
                wim[rows, imag] = cosine
                wim[rows, real] = sine.astype(jnp.bfloat16)
                wre[rows, imag] = (-sine).astype(jnp.bfloat16)
        return carry

    lax.fori_loop(0, FEEDS // 128, table, 0)
    blocks = BEAMS // 256
    lane = lax.broadcasted_iota(jnp.int32, (16, 128), 1)
    on = {w: (lane & w) != 0 for w in (16, 32, 64)}


    def finish(q, nb):
        for o in range(4):
            parts = []
            for g in range(4):
                at = pl.ds(pl.multiple_of(nb * 256 + o * 64 + g * 16, 16), 16)
                real = sums[q, 0, at, :]
                imag = sums[q, 1, at, :]
                power = real * real + imag * imag
                parts.append(power[:, :128] + power[:, 128:])
            halves = [
                jnp.where(on[64], b, a) + pltpu.roll(jnp.where(on[64], a, b), 64, 1)
                for a, b in ((parts[0], parts[2]), (parts[1], parts[3]))
            ]
            other = jnp.where(on[32], halves[0], halves[1])
            total = jnp.where(on[32], halves[1], halves[0]) + jnp.where(
                on[32], pltpu.roll(other, 32, 1), pltpu.roll(other, 96, 1)
            )
            pbuf[nb * 4 + o, q] = encode(total)

    def add(q, nb, first, tiles, fresh):
        rows = pl.ds(pl.multiple_of(nb * 256, 256), 256)
        terms = pl.ds(pl.multiple_of(first * 256, 256), tiles * 256)
        feeds = recv[q, pl.ds(first, tiles)].reshape(tiles * 256, 256)
        for r, weights in enumerate((wre, wim)):
            part = jnp.dot(weights[rows, terms], feeds, preferred_element_type=jnp.float32)
            sums[q, r, rows, :] = part if fresh else sums[q, r, rows, :] + part

    def beams(body):
        def one(i, carry):
            body(lax.rem(i + (1 - me // 8) * 2, blocks))
            return carry

        lax.fori_loop(0, blocks, one, 0)

    each(volt_copy, "start", 1, (8, 12, 1, 9, 13, 2, 10, 14, 3, 11, 15, 4, 5, 6, 7))
    near = me // 8 * 4
    far = (flip(me, 8) // 4 * 2, flip(me, 12) // 4 * 2)
    for g in range(2):
        own_copy(g).wait()
        each(volt_copy, "wait_recv", g, range(1, 8))
        for q in range(GROUPS[g][0], sum(GROUPS[g])):
            beams(lambda nb, q=q: add(q, nb, near, 4, True))
    each(volt_copy, "wait_recv", 0, range(8, 12))
    for q in range(3):
        beams(lambda nb, q=q: add(q, nb, far[0], 2, False))
    each(volt_copy, "wait_recv", 0, range(12, 16))
    for q in range(3):

        def whole(nb, q=q):
            add(q, nb, far[1], 2, False)
            finish(q, nb)

        beams(whole)
    each(power_copy, "start", 0, (12, 13, 14, 15, 8, 9, 10, 11, 1, 2, 3, 4, 5, 6, 7))
    own_power(0).start()
    each(volt_copy, "wait_recv", 1, range(8, 12))
    beams(lambda nb: add(3, nb, far[0], 2, False))
    each(volt_copy, "wait_recv", 1, range(12, 16))

    def last(nb):
        add(3, nb, far[1], 2, False)
        finish(3, nb)
        for o in range(4):
            m = flip(me, nb * 4 + o)

            @pl.when(m > 0)
            def _(m=m):
                power_copy(1, m).start()

    beams(last)
    own_power(1).start()
    each(volt_copy, "wait_send", 0)
    each(volt_copy, "wait_send", 1)

    for h in range(2):
        each(power_copy, "wait_send", h)
        each(power_copy, "wait_recv", h)
        own_power(h).wait()
        tiles = []
        for t in range(4):
            vals = [
                decode(precv[4 * t + s, h * 2 + c]) for s in range(4) for c in range(2)
            ]
            for b in range(3):
                w = 16 << b
                for a in range(8):
                    if not a >> b & 1:
                        z = a | 1 << b
                        vals[a], vals[z] = (
                            jnp.where(on[w], pltpu.roll(vals[z], w, 1), vals[a]),
                            jnp.where(on[w], vals[z], pltpu.roll(vals[a], 128 - w, 1)),
                        )
            tiles.append(vals)
        for a in range(8):
            total = tiles[0][a] + tiles[1][a] + tiles[2][a] + tiles[3][a]
            baseline = jnp.sum(total, axis=1, keepdims=True) * (1.0 / (n * 32))
            scale = 1.0 / (baseline + eps_power * TWIDDLE_GAIN**2)
            for t in range(4):
                at = (a >> 1) * 256 + t * 4 + h * 2 + (a & 1)
                out_ref[pl.ds(at, 16, stride=16), :] = tiles[t][a] * scale


def fused(n, voltages, gains, feed_cyl, feed_ns, ew_index, ns_beam):
    vmem = pl.BlockSpec(memory_space=pltpu.VMEM)
    dma = pltpu.SemaphoreType.DMA
    out = pl.pallas_call(
        functools.partial(beam_kernel, n),
        out_shape=pltpu.VMEM((1024, 128), jnp.float32),
        in_specs=[
            pl.BlockSpec(memory_space=pl.ANY), vmem, vmem, vmem,
            pl.BlockSpec(memory_space=pltpu.SMEM), vmem,
        ],
        out_specs=vmem,
        scratch_shapes=[
            pltpu.VMEM(voltages.shape, jnp.bfloat16),
            pltpu.VMEM((2, 2, 2, 64 * 2 * n, 128), jnp.float32),
            pltpu.VMEM((2, 2, 64, 128), jnp.float32),
            pltpu.VMEM((NSB, 128), jnp.int32),
            pltpu.VMEM((256, 256), jnp.bfloat16),
            pltpu.VMEM((512, 256), jnp.bfloat16),
            pltpu.VMEM((n, PIECES, 2, 64, 256), jnp.bfloat16),
            pltpu.VMEM((PIECES, n // 2, 2, 2, 64, 256), jnp.bfloat16),
            pltpu.VMEM((BEAMS, 2 * FEEDS), jnp.bfloat16),
            pltpu.VMEM((BEAMS, 2 * FEEDS), jnp.bfloat16),
            pltpu.VMEM((PIECES, 2, BEAMS, 256), jnp.float32),
            pltpu.VMEM((n, PIECES, 16, 128), jnp.bfloat16),
            pltpu.VMEM((n, PIECES, 16, 128), jnp.bfloat16),
            dma((8,)), dma((2, n)), dma((2, n)), dma((2,)),
            dma((2, n)), dma((2, n)), dma((2,)),
        ],
        compiler_params=pltpu.CompilerParams(
            collective_id=0, has_side_effects=True, vmem_limit_bytes=56 << 20
        ),
    )(
        voltages, gains, feed_cyl.reshape(-1, 128), feed_ns.reshape(-1, 128),
        ew_index, ns_beam.reshape(-1, 128),
    )
    return out.reshape(64, 4, TOUT, 128).transpose(0, 2, 1, 3).reshape(64, TOUT, 512)


def solution(mesh):
    placed = (P(None, "chan", None, None, "grp"), P(None, None, "chan"), P(), P(), P(), P())
    n = mesh.shape["chan"]

    def part(voltages, gains, feed_cyl, feed_ns, ew_index, ns_beam):
        fits = voltages.shape == (2, 64, 2, 2 * n, UP * DS * TOUT) and n * 64 == FEEDS
        run = functools.partial(fused, n) if fits else shards
        return run(voltages, gains, feed_cyl, feed_ns, ew_index, ns_beam)

    return jax.shard_map(
        part, mesh=mesh, in_specs=placed, out_specs=P("chan", "grp", None), check_vma=False
    )
```

```python
import functools
import math

import jax
import jax.numpy as jnp
from jax import lax
from jax.experimental import pallas as pl
from jax.experimental.pallas import tpu as pltpu
from jax.sharding import PartitionSpec as P

CYL = 4
NSF = 256
EWB = 4
NSB = 256
EW_PH = 64
UP = 16
DS = 4
FEEDS = 1024
BEAMS = 1024
TOUT = 4


eps_power = 1e-06
MESH = pl.DeviceIdType.MESH
PIECES = 4
EARLY = 1
GROUPS = ((0, 3), (3, 1))
ORDER = (8, 9, 10, 11, 12, 13, 14, 15, 1, 2, 3, 4, 5, 6, 7)
TWIDDLE = 1.1305
TWIDDLE_GAIN = 1.132804


def phase_table(feed_cyl, feed_ns, ew_index, ns_beam):
    modulus = 2 * NSF * EW_PH
    cyl_onehot = (feed_cyl[:, None] == jnp.arange(CYL, dtype=jnp.int32)[None, :]).astype(jnp.int32)
    ew_term = jnp.sum(cyl_onehot[:, None, :] * ew_index[None, :, :], axis=2)
    ns_term = feed_ns[:, None] * ns_beam[None, :] * EW_PH
    steps_int = (ew_term[:, :, None] * (2 * NSF) + ns_term[:, None, :]) % modulus
    angles = steps_int.reshape(FEEDS, EWB * NSB).astype(jnp.float32) * (2.0 * math.pi / modulus)
    cosine = jnp.cos(angles).astype(jnp.bfloat16)
    sine_part = jnp.sin(angles).astype(jnp.bfloat16)
    upper_rows = jnp.concatenate([cosine, sine_part], axis=1)
    lower_rows = jnp.concatenate([-sine_part, cosine], axis=1)
    return jnp.concatenate([upper_rows, lower_rows], axis=0)


def upchannel_table():
    bin_index = jnp.arange(UP, dtype=jnp.int32)
    angles = (bin_index[:, None] * bin_index[None, :] % UP).astype(jnp.float32) * (
        2.0 * math.pi / UP
    )
    cosine = jnp.cos(angles)
    sine_part = jnp.sin(angles)
    return jnp.stack([jnp.stack([cosine, -sine_part], -1), jnp.stack([sine_part, cosine], -1)], 1)


def shards(voltages, gains, feed_cyl, feed_ns, ew_index, ns_beam):
    weights = phase_table(feed_cyl, feed_ns, ew_index, ns_beam).reshape(2, FEEDS, 2 * BEAMS)
    fine_table = upchannel_table()
    sample = voltages.astype(jnp.float32)
    gain_real = gains[0].T[:, :, None, None]
    gain_imag = gains[1].T[:, :, None, None]
    calibrated = jnp.stack(
        [
            (gain_real * sample[0] - gain_imag * sample[1]).astype(jnp.bfloat16),
            (gain_real * sample[1] + gain_imag * sample[0]).astype(jnp.bfloat16),
        ]
    )
    arrived = lax.all_to_all(calibrated, "chan", split_axis=3, concat_axis=1, tiled=True)
    pieces = arrived.shape[2]
    channels = arrived.shape[3]
    beam_sums = jnp.einsum("rfpct,rfq->pctq", arrived, weights, preferred_element_type=jnp.float32)
    beam_sums = beam_sums.reshape(pieces, channels, TOUT, DS, UP, 2, BEAMS)
    fine_bins = jnp.einsum(
        "pcudjrb,jrks->pbudcks", beam_sums, fine_table, precision=lax.Precision.HIGHEST
    )
    beam_power = jnp.sum(jnp.sum(fine_bins * fine_bins, axis=(3, 6)), axis=0)
    total_chans = beam_power.shape[2] * lax.axis_size("chan")
    band_sum = lax.psum(jnp.sum(beam_power, axis=(2, 3)), "chan")
    baseline = band_sum / (total_chans * UP)
    normed = beam_power / (baseline[:, :, None, None] + eps_power)
    intensity = lax.all_to_all(normed, "chan", split_axis=0, concat_axis=2, tiled=True)
    return intensity.reshape(intensity.shape[0], TOUT, intensity.shape[2] * UP)


def cos_sin(steps):
    quarter = (steps + 64) >> 7
    x = (steps - (quarter << 7)).astype(jnp.float32) * (2.0 * math.pi / 512)
    y = x * x
    s = x * (1.0 + y * (-1 / 6 + y * (1 / 120 + y * (-1 / 5040 + y * (1 / 362880)))))
    c = 1.0 + y * (-0.5 + y * (1 / 24 + y * (-1 / 720 + y * (1 / 40320))))
    odd = (quarter & 1) == 1
    cosine = jnp.where(odd, s, c)
    sine = jnp.where(odd, c, s)
    cosine = jnp.where(((quarter + 1) & 2) == 2, -cosine, cosine)
    sine = jnp.where((quarter & 2) == 2, -sine, sine)
    return cosine, sine


def encode(power):
    small = power < 2.0**-17
    scaled = jnp.where(small, power * -(2.0**80), power * 2.0**17)
    return (scaled * jnp.abs(scaled)).astype(jnp.bfloat16)


def decode(code):
    code = code.astype(jnp.float32)
    size = jnp.abs(code)
    root = size * lax.rsqrt(jnp.maximum(size, 2.0**-126))
    return root * jnp.where(code < 0, 2.0**-80, 2.0**-17)


def flip(me, m):
    bits = [lax.rem(me // b + m // b, 2) * b for b in (1, 2, 4, 8)]
    return bits[0] + bits[1] + bits[2] + bits[3]


def beam_kernel(
    n, volt_ref, gain_ref, cyl_ref, ns_ref, ew_ref, nb_ref, out_ref,
    volt, wide, gcol, ncol, dft, xin, x_ref,
    recv, wre, wim, sums, pbuf, precv,
    volt_sem, send_sem, recv_sem, own_sem, psend_sem, precv_sem, pown_sem,
):
    me = lax.axis_index("chan")

    def fetch(i):
        feeds = pl.ds(pl.multiple_of(i * 8, 8), 8)
        return pltpu.make_async_copy(volt_ref.at[:, feeds], volt.at[:, feeds], volt_sem.at[i])

    def begin(i, carry):
        fetch(i).start()
        return carry

    lax.fori_loop(0, 8, begin, 0)
    barrier = pltpu.get_barrier_semaphore()

    def greet(s, carry):
        pl.semaphore_signal(
            barrier, inc=1, device_id={"chan": lax.rem(me + s, n)}, device_id_type=MESH
        )
        return carry

    lax.fori_loop(1, n, greet, 0)

    row = lax.broadcasted_iota(jnp.int32, dft.shape, 0)
    col = lax.broadcasted_iota(jnp.int32, dft.shape, 1)
    same = (((row >> 6) & 1) == ((col >> 4) & 1)) & (((row >> 4) & 3) == ((col >> 5) & 3))
    turns = (row & 15) * (col & 15) * 32 + ((col >> 7) - (row >> 7)) * 128
    dft[...] = jnp.where(same, cos_sin(turns & 511)[0] * TWIDDLE, 0.0).astype(jnp.bfloat16)
    for r in range(2):
        for p in range(2):
            gcol[r, p] = jnp.broadcast_to(gain_ref[r, p : p + 1, :], (128, 64)).T

    def widen(i, carry):
        fetch(i).wait()
        first = pl.multiple_of(i * 8 * 2 * n, 8 * 2 * n)
        for r in range(2):
            for p in range(2):
                part = volt[r, pl.ds(pl.multiple_of(i * 8, 8), 8), p].astype(jnp.float32)
                part = part.reshape(8 * 2 * n, 256)
                for h in range(2):
                    wide[r, p, h, pl.ds(first, 8 * 2 * n), :] = part[:, h * 128 : (h + 1) * 128]
        return carry

    lax.fori_loop(0, 8, widen, 0)

    def volt_copy(g, m):
        d = flip(me, m)
        return pltpu.make_async_remote_copy(
            src_ref=x_ref.at[d, pl.ds(*GROUPS[g])],
            dst_ref=recv.at[pl.ds(*GROUPS[g]), me // 2, :, lax.rem(me, 2)],
            send_sem=send_sem.at[g, m],
            recv_sem=recv_sem.at[g, m],
            device_id={"chan": d},
            device_id_type=MESH,
        )

    def own_copy(g):
        return pltpu.make_async_copy(
            x_ref.at[me, pl.ds(*GROUPS[g])],
            recv.at[pl.ds(*GROUPS[g]), me // 2, :, lax.rem(me, 2)],
            own_sem.at[g],
        )

    def power_copy(g, m):
        d = flip(me, m)
        return pltpu.make_async_remote_copy(
            src_ref=pbuf.at[d, pl.ds(*GROUPS[g])],
            dst_ref=precv.at[me, pl.ds(*GROUPS[g])],
            send_sem=psend_sem.at[g, m],
            recv_sem=precv_sem.at[g, m],
            device_id={"chan": d},
            device_id_type=MESH,
        )

    def own_power(g):
        return pltpu.make_async_copy(
            pbuf.at[me, pl.ds(*GROUPS[g])], precv.at[me, pl.ds(*GROUPS[g])], pown_sem.at[g]
        )

    def partner(i):
        return (1 - i // 8) * (8 + i) + i // 8 * lax.rem(i + 1, 8)

    def each(make, act, g, partners=ORDER):
        for m in partners:
            getattr(make(g, m), act)()

    def produce(i, carry):
        m = partner(i)
        d = flip(me, m)
        for p in range(2):
            gr = gcol[0, p]
            gi = gcol[1, p]
            for c in range(2):
                for h in range(2):
                    at = pl.ds(d * 2 + c, 64, stride=2 * n)
                    real = wide[0, p, h, at, :]
                    imag = wide[1, p, h, at, :]
                    first = ((h * 2 + c) * 2 + p) * 64
                    xin[first : first + 64, :128] = (gr * real - gi * imag).astype(jnp.bfloat16)
                    xin[first : first + 64, 128:] = (gr * imag + gi * real).astype(jnp.bfloat16)
        bins = jnp.dot(xin[...], dft[...], preferred_element_type=jnp.float32)
        for q in range(PIECES):
            for p in range(2):
                part = bins[(q * 2 + p) * 64 : (q * 2 + p) * 64 + 64].astype(jnp.bfloat16)
                for r in range(2):
                    x_ref[d, q, r, :, p * 128 : (p + 1) * 128] = part[:, r * 128 : (r + 1) * 128]

        return carry

    def produce_and_send(i, carry):
        produce(i, carry)

        @pl.when(i < n - 1)
        def _():
            volt_copy(0, partner(i)).start()

        return carry

    lax.fori_loop(0, EARLY, produce, 0)
    pl.semaphore_wait(barrier, n - 1)
    each(volt_copy, "start", 0, ORDER[:EARLY])
    lax.fori_loop(EARLY, n, produce_and_send, 0)
    for g in range(2):
        own_copy(g).start()

    for h in range(2):
        ncol[h * 128 : (h + 1) * 128, :] = jnp.broadcast_to(nb_ref[h : h + 1, :], (128, 128)).T

    def table(i, carry):
        real = pl.ds(pl.multiple_of(i * 256, 256), 128)
        imag = pl.ds(pl.multiple_of(i * 256 + 128, 128), 128)
        cyl = cyl_ref[pl.ds(i, 1), :]
        ns = jnp.broadcast_to(ns_ref[pl.ds(i, 1), :], (128, 128))
        for h in range(2):
            slope = ns * ncol[h * 128 : (h + 1) * 128, :]
            for e in range(EWB):
                shift = jnp.where(
                    cyl < 2,
                    jnp.where(cyl == 0, ew_ref[e, 0], ew_ref[e, 1]),
                    jnp.where(cyl == 2, ew_ref[e, 2], ew_ref[e, 3]),
                )
                cosine, sine = cos_sin((slope + shift * 8) & 511)
                rows = slice(e * NSB + h * 128, e * NSB + h * 128 + 128)
                cosine = cosine.astype(jnp.bfloat16)
                wre[rows, real] = cosine
                wim[rows, imag] = cosine
                wim[rows, real] = sine.astype(jnp.bfloat16)
                wre[rows, imag] = (-sine).astype(jnp.bfloat16)
        return carry

    lax.fori_loop(0, FEEDS // 128, table, 0)
    blocks = BEAMS // 256
    lane = lax.broadcasted_iota(jnp.int32, (16, 128), 1)
    on = {w: (lane & w) != 0 for w in (16, 32, 64)}


    def finish(q, nb):
        for o in range(4):
            parts = []
            for g in range(4):
                at = pl.ds(pl.multiple_of(nb * 256 + o * 64 + g * 16, 16), 16)
                real = sums[q, 0, at, :]
                imag = sums[q, 1, at, :]
                power = real * real + imag * imag
                parts.append(power[:, :128] + power[:, 128:])
            halves = [
                jnp.where(on[64], b, a) + pltpu.roll(jnp.where(on[64], a, b), 64, 1)
                for a, b in ((parts[0], parts[2]), (parts[1], parts[3]))
            ]
            other = jnp.where(on[32], halves[0], halves[1])
            total = jnp.where(on[32], halves[1], halves[0]) + jnp.where(
                on[32], pltpu.roll(other, 32, 1), pltpu.roll(other, 96, 1)
            )
            pbuf[nb * 4 + o, q] = encode(total)

    def add(q, nb, first, tiles, fresh):
        rows = pl.ds(pl.multiple_of(nb * 256, 256), 256)
        terms = pl.ds(pl.multiple_of(first * 256, 256), tiles * 256)
        feeds = recv[q, pl.ds(first, tiles)].reshape(tiles * 256, 256)
        for r, weights in enumerate((wre, wim)):
            part = jnp.dot(weights[rows, terms], feeds, preferred_element_type=jnp.float32)
            sums[q, r, rows, :] = part if fresh else sums[q, r, rows, :] + part

    def beams(body):
        def one(i, carry):
            body(lax.rem(i + (1 - me // 8) * 2, blocks))
            return carry

        lax.fori_loop(0, blocks, one, 0)

    each(volt_copy, "start", 1, (8, 12, 1, 9, 13, 2, 10, 14, 3, 11, 15, 4, 5, 6, 7))
    near = me // 8 * 4
    far = (flip(me, 8) // 4 * 2, flip(me, 12) // 4 * 2)
    for g in range(2):
        own_copy(g).wait()
        each(volt_copy, "wait_recv", g, range(1, 8))
        for q in range(GROUPS[g][0], sum(GROUPS[g])):
            beams(lambda nb, q=q: add(q, nb, near, 4, True))
    each(volt_copy, "wait_recv", 0, range(8, 12))
    for q in range(3):
        beams(lambda nb, q=q: add(q, nb, far[0], 2, False))
    each(volt_copy, "wait_recv", 0, range(12, 16))
    for q in range(3):

        def whole(nb, q=q):
            add(q, nb, far[1], 2, False)
            finish(q, nb)

        beams(whole)
    each(power_copy, "start", 0, (12, 13, 14, 15, 8, 9, 10, 11, 1, 2, 3, 4, 5, 6, 7))
    own_power(0).start()
    each(volt_copy, "wait_recv", 1, range(8, 12))
    beams(lambda nb: add(3, nb, far[0], 2, False))
    each(volt_copy, "wait_recv", 1, range(12, 16))

    def last(nb):
        add(3, nb, far[1], 2, False)
        finish(3, nb)
        for o in range(4):
            m = flip(me, nb * 4 + o)

            @pl.when(m > 0)
            def _(m=m):
                power_copy(1, m).start()

    beams(last)
    own_power(1).start()
    each(volt_copy, "wait_send", 0)
    each(volt_copy, "wait_send", 1)

    for h in range(2):
        each(power_copy, "wait_send", h)
        each(power_copy, "wait_recv", h)
        own_power(h).wait()
        tiles = []
        for t in range(4):
            vals = [
                decode(precv[4 * t + s, h * 2 + c]) for s in range(4) for c in range(2)
            ]
            for b in range(3):
                w = 16 << b
                for a in range(8):
                    if not a >> b & 1:
                        z = a | 1 << b
                        vals[a], vals[z] = (
                            jnp.where(on[w], pltpu.roll(vals[z], w, 1), vals[a]),
                            jnp.where(on[w], vals[z], pltpu.roll(vals[a], 128 - w, 1)),
                        )
            tiles.append(vals)
        for a in range(8):
            total = tiles[0][a] + tiles[1][a] + tiles[2][a] + tiles[3][a]
            baseline = jnp.sum(total, axis=1, keepdims=True) * (1.0 / (n * 32))
            scale = 1.0 / (baseline + eps_power * TWIDDLE_GAIN**2)
            for t in range(4):
                at = (a >> 1) * 256 + t * 4 + h * 2 + (a & 1)
                out_ref[pl.ds(at, 16, stride=16), :] = tiles[t][a] * scale


def fused(n, voltages, gains, feed_cyl, feed_ns, ew_index, ns_beam):
    vmem = pl.BlockSpec(memory_space=pltpu.VMEM)
    dma = pltpu.SemaphoreType.DMA
    out = pl.pallas_call(
        functools.partial(beam_kernel, n),
        out_shape=pltpu.VMEM((1024, 128), jnp.float32),
        in_specs=[
            pl.BlockSpec(memory_space=pl.ANY), vmem, vmem, vmem,
            pl.BlockSpec(memory_space=pltpu.SMEM), vmem,
        ],
        out_specs=vmem,
        scratch_shapes=[
            pltpu.VMEM(voltages.shape, jnp.bfloat16),
            pltpu.VMEM((2, 2, 2, 64 * 2 * n, 128), jnp.float32),
            pltpu.VMEM((2, 2, 64, 128), jnp.float32),
            pltpu.VMEM((NSB, 128), jnp.int32),
            pltpu.VMEM((256, 256), jnp.bfloat16),
            pltpu.VMEM((512, 256), jnp.bfloat16),
            pltpu.VMEM((n, PIECES, 2, 64, 256), jnp.bfloat16),
            pltpu.VMEM((PIECES, n // 2, 2, 2, 64, 256), jnp.bfloat16),
            pltpu.VMEM((BEAMS, 2 * FEEDS), jnp.bfloat16),
            pltpu.VMEM((BEAMS, 2 * FEEDS), jnp.bfloat16),
            pltpu.VMEM((PIECES, 2, BEAMS, 256), jnp.float32),
            pltpu.VMEM((n, PIECES, 16, 128), jnp.bfloat16),
            pltpu.VMEM((n, PIECES, 16, 128), jnp.bfloat16),
            dma((8,)), dma((2, n)), dma((2, n)), dma((2,)),
            dma((2, n)), dma((2, n)), dma((2,)),
        ],
        compiler_params=pltpu.CompilerParams(
            collective_id=0, has_side_effects=True, vmem_limit_bytes=56 << 20
        ),
    )(
        voltages, gains, feed_cyl.reshape(-1, 128), feed_ns.reshape(-1, 128),
        ew_index, ns_beam.reshape(-1, 128),
    )
    return out.reshape(64, 4, TOUT, 128).transpose(0, 2, 1, 3).reshape(64, TOUT, 512)


def solution(mesh):
    placed = (P(None, "chan", None, None, "grp"), P(None, None, "chan"), P(), P(), P(), P())
    n = mesh.shape["chan"]

    def part(voltages, gains, feed_cyl, feed_ns, ew_index, ns_beam):
        fits = voltages.shape == (2, 64, 2, 2 * n, UP * DS * TOUT) and n * 64 == FEEDS
        run = functools.partial(fused, n) if fits else shards
        return run(voltages, gains, feed_cyl, feed_ns, ew_index, ns_beam)

    return jax.shard_map(
        part, mesh=mesh, in_specs=placed, out_specs=P("chan", "grp", None), check_vma=False
    )
```
